512 devices in a mesh: dp: 32 (over z, x_lo), seq: 16 (over x_hi, y, core).
Axes of the slice: x: 4 (x_hi: 2, x_lo: 2; x = x_hi * 2 + x_lo), y: 4, z: 16, core: 2. Of those that a mesh axis runs over, the one named last changes fastest.
Arguments:
- tokens: bfloat16 [32, 2048, 8192], P('dp', 'seq'), may hold values from -6 to 6
- gain: float32 [8192], replicated, may hold values from 0.25 to 1.75
- w_t: bfloat16 [512, 8192], P('dp', 'seq'), may hold values from -0.0625 to 0.0625
- grad_values: bfloat16 [32, 2048, 512], P('dp', 'seq'), may hold values from -6 to 6
- owner: int32 [512], replicated, may hold values from 0 to 31, as said below
- master: float32 [32, 32, 8192], P('dp', None, 'seq'), may hold values from -0.0625 to 0.0625
- moment1: float32 [32, 32, 8192], P('dp', None, 'seq'), may hold values from -0.024 to 0.024
- moment2: float32 [32, 32, 8192], P('dp', None, 'seq'), may hold values from 1e-06 to 4e-05
Outputs:
- values: bfloat16 [32, 2048, 512], P('dp', 'seq')
- grad_x: bfloat16 [32, 2048, 8192], P('dp', 'seq')
- new_master: float32 [32, 32, 8192], P('dp', None, 'seq')
- new_moment1: float32 [32, 32, 8192], P('dp', None, 'seq')
- new_moment2: float32 [32, 32, 8192], P('dp', None, 'seq')
The draws below stay inside these ranges and needn't reach their ends.
Inputs may be any that keep to these rules, and one draw needn't show every extreme that they name: `owner`: each index of dp owns at most 32 rows and some own exactly 32; some may own none.
All inputs are finite; a program needn't handle non-finite values.
Results may differ from the reference program's by a relative error of at most 0.012.
Values may be sent and summed in bfloat16 or wider, within the bound.
A program may use at most 128 MiB of HBM per device.

```python
import math
import jax
import jax.numpy as jnp
from jax import lax

D = 8192
F = 512
LEN = 2048
CAP = 32
N_DP = 32


def draw_owner(key, part):
    first_key, second_key = jax.random.split(jax.random.fold_in(key, 11))
    pair_count = max(N_DP // 8, 1)
    row_order = jax.random.permutation(first_key, F)
    row_label = row_order % N_DP
    row_label = jnp.where((row_label >= pair_count) & (row_label < 2 * pair_count), row_label - pair_count, row_label)
    device_order = jax.random.permutation(second_key, N_DP)
    return device_order[row_label].astype(jnp.int32)


def strengthened(values, key, source, target, blocks, factor):
    def block_of(dim):
        return (jnp.arange(values.shape[dim]) // (values.shape[dim] // blocks)).reshape((-1,) + (1,) * (values.ndim - 1 - dim))

    near = jax.random.permutation(key, blocks)[block_of(target)]
    other_side = (block_of(target) + blocks // 2) % blocks
    return jnp.where((block_of(source) == near) | (block_of(source) == other_side), factor * values, values)


def shard_levels(stream_key, shape, cuts, smallest, largest):
    level = 1.0
    for axis_at, parts in cuts:
        draws = jax.random.uniform(jax.random.fold_in(jax.random.fold_in(stream_key, 6), axis_at), (parts,), jnp.float32, smallest / len(cuts), largest / len(cuts))
        level = level * jnp.repeat(jnp.exp(draws), shape[axis_at] // parts).reshape((-1,) + (1,) * (len(shape) - 1 - axis_at))
    return level


def bell_draw(own_key, shape, scale, most, pieces=(), held_as=jnp.bfloat16):
    entries = jax.random.normal(own_key, shape, jnp.float32) * scale
    if len(pieces) > 0:
        entries = shard_levels(own_key, shape, pieces, -0.22, 0.18) * entries
    return jnp.clip(entries, min=-most, max=most).astype(held_as)


def gaussian_with(own_key, shape, deviation, reach, cuts, heavy, kind=jnp.bfloat16):
    array = deviation * jax.random.normal(own_key, shape, jnp.float32)
    if cuts:
        array = array * shard_levels(own_key, shape, cuts, -0.22, 0.18)
    return jnp.clip(strengthened(array, jax.random.fold_in(own_key, 3), *heavy), -reach, reach).astype(kind)


def setup_inputs(seed: int = 0) -> dict:
    streams_of = jax.random.split(jax.random.key(seed), 9)
    tokens = bell_draw(streams_of[0], (N_DP, LEN, D), 1.0, 6.0, ((0, 32), (1, 16)))
    gain = jnp.clip(1.0 + 0.15 * jax.random.normal(streams_of[1], (D,), jnp.float32), 0.25, 1.75)
    w_t = bell_draw(streams_of[2], (F, D), D ** -0.5, 0.0625, ((0, 32), (1, 16)))
    grad_values = gaussian_with(streams_of[3], (N_DP, LEN, F), 1.0, 6.0, ((0, 32), (1, 16)), (0, 2, 32, 2.75))
    owner = draw_owner(jax.random.fold_in(streams_of[8], 71), 0)
    master = bell_draw(streams_of[5], (N_DP, CAP, D), D ** -0.5, 0.0625, ((0, 32), (2, 16)), jnp.float32)
    moment1 = bell_draw(streams_of[6], (N_DP, CAP, D), 0.004, 0.024, ((0, 32), (2, 16)), jnp.float32)
    moment2 = jnp.clip(jnp.exp(math.log(3.9999998989515007e-05) - 3.6888794 * jax.random.uniform(streams_of[7], (N_DP, CAP, D), jnp.float32) ** shard_levels(streams_of[7], (N_DP, CAP, D), ((0, 32), (2, 16)), -0.2, 0.2)), 9.999999974752427e-07, 3.9999998989515007e-05)
    return {"tokens": tokens, "gain": gain, "w_t": w_t, "grad_values": grad_values, "owner": owner, "master": master, "moment1": moment1, "moment2": moment2}


beta_one = 0.9
beta_two = 0.95
learn_rate = 0.001
adam_eps = 1e-08
bias_one = 1.0 - 0.9 ** 10
bias_two = 1.0 - 0.95 ** 10

def reference(tokens, gain, w_t, grad_values, owner, master, moment1, moment2):

    def one_sequence(carry, inputs):
        seq_tokens, seq_grads = inputs
        tok_float = seq_tokens.astype(jnp.float32)
        inv_rms = lax.rsqrt(lax.optimization_barrier(jnp.mean(tok_float * tok_float, axis=-1, keepdims=True)) + 1e-05)
        scaled = tok_float * inv_rms
        normed = (scaled * gain).astype(jnp.bfloat16)
        values = lax.dot_general(normed, w_t, (((1,), (1,)), ((), ())), preferred_element_type=jnp.float32).astype(jnp.bfloat16)
        grad_normed = jnp.dot(seq_grads, w_t, preferred_element_type=jnp.float32).astype(jnp.bfloat16)
        weighted = gain * grad_normed.astype(jnp.float32)
        grad_x = (inv_rms * (weighted - scaled * lax.optimization_barrier(jnp.mean(weighted * scaled, axis=-1, keepdims=True)))).astype(jnp.bfloat16)
        block = lax.dot_general(seq_grads, normed, (((0,), (0,)), ((), ())), preferred_element_type=jnp.float32)
        return (carry + block, (values, grad_x))
    summed, outputs = lax.scan(one_sequence, jnp.zeros((F, D), jnp.float32), (tokens, grad_values))
    values, grad_x = outputs
    weight_grad = summed / (LEN * N_DP)
    onehot = (owner[:, None] == jnp.arange(N_DP, dtype=jnp.int32)[None, :]).astype(jnp.int32)
    prior_count = jnp.cumsum(onehot, axis=0) - onehot
    slot_row = lax.optimization_barrier(jnp.sum(prior_count * onehot, axis=1))
    select_all = ((owner[None, None, :] == jnp.arange(N_DP, dtype=jnp.int32)[:, None, None]) & (slot_row[None, None, :] == jnp.arange(CAP, dtype=jnp.int32)[None, :, None])).astype(jnp.float32)
    slot_grad = jnp.einsum('pjf,fd->pjd', select_all, weight_grad, precision=lax.Precision.HIGHEST)
    occupied = lax.optimization_barrier(jnp.sum(select_all, axis=-1, keepdims=True))
    new_moment1 = (beta_one * moment1 + (1.0 - beta_one) * slot_grad) * occupied
    new_moment2 = (beta_two * moment2 + (1.0 - beta_two) * slot_grad * slot_grad) * occupied
    step_dir = new_moment1 / bias_one / (jnp.sqrt(new_moment2 / bias_two) + adam_eps)
    new_master = (master - learn_rate * step_dir) * occupied
    return (values, grad_x, new_master, new_moment1, new_moment2)
```

```python
import jax
import jax.numpy as jnp
from jax import lax
from jax.experimental import pallas as pl
from jax.experimental.pallas import tpu as pltpu
from jax.sharding import PartitionSpec as P

beta_one = 0.9
beta_two = 0.95
learn_rate = 0.001
adam_eps = 1e-08
bias_one = 1.0 - 0.9**10
bias_two = 1.0 - 0.95**10

MESH = pl.DeviceIdType.MESH
f32, bf16 = jnp.float32, jnp.bfloat16


def kernel(
    tok_ref, gain_ref, w_ref, gv_ref, pos_ref,
    val_ref, gn_ref, inv_ref, mean_ref, sg_ref,
    W, N, GA, GB, RA, RB, QA, QB, RQA, RQB, PM, ZS, RZ, C, RZ2, vacc, racc,
    ssem, rsem,
):
    dp, seq = lax.axis_index("dp"), lax.axis_index("seq")
    z, xl = dp // 2, dp % 2
    xh, y, c = seq // 8, (seq // 2) % 4, seq % 2
    x = 2 * xh + xl
    a, b = z // 4, z % 4

    def at(z_=None, x_=None, y_=None, c_=None):
        z_ = z if z_ is None else z_
        x_ = x if x_ is None else x_
        y_ = y if y_ is None else y_
        c_ = c if c_ is None else c_
        return (2 * z_ + x_ % 2, 8 * (x_ // 2) + 2 * y_ + c_)

    def zoff(k):
        return (z + k) % 16

    def aoff(k):
        return 4 * ((a + k) % 4) + b

    xn = x + 1 - 2 * xl

    barrier = pltpu.get_barrier_semaphore()
    peers = [at(z_=zoff(k)) for k in (1, 15, 2, 14, 4, 8, 12)]
    peers += [at(z_=aoff(k), x_=xn) for k in (1, 2, 3)]
    peers += [at(y_=(y + k) % 4, c_=(c + m) % 2) for k in range(4) for m in range(2) if (k, m) != (0, 0)]
    peers += [at(x_=(x + k) % 4, c_=(c + m) % 2) for k in (1, 2, 3) for m in range(2)]
    for peer in peers:
        pl.semaphore_signal(barrier, inc=1, device_id=peer, device_id_type=MESH)
    pl.semaphore_wait(barrier, len(peers))

    sent = []

    def send(src, dst, to):
        k = len(sent)
        copy = pltpu.make_async_remote_copy(
            src_ref=src, dst_ref=dst, send_sem=ssem.at[k], recv_sem=rsem.at[k],
            device_id=to, device_id_type=MESH,
        )
        copy.start()
        sent.append(copy)
        return copy

    def arrived(copies):
        for copy in copies:
            copy.wait_recv()

    ja, jb = 2 * y + c, 2 * x + c

    for h in range(2):
        W[xh, y, c, h, a, b, xl] = w_ref[:, 256 * h : 256 * h + 256]
    w_one = []
    for k in (1, 3, 2):
        part = W.at[xh, y, c, :, a, b, xl]
        w_one.append(send(part, part, at(z_=aoff(k))))

    g_a, g_b = [], []
    for k in range(4):
        for m in range(2):
            if (k, m) != (0, 0):
                g_a.append(send(gv_ref, GA.at[ja], at(y_=(y + k) % 4, c_=(c + m) % 2)))
                g_b.append(send(gv_ref, GB.at[jb], at(x_=(x + k) % 4, c_=(c + m) % 2)))
    GA[ja] = gv_ref[...]
    GB[jb] = gv_ref[...]

    def square(i, total):
        t = tok_ref[:, pl.ds(pl.multiple_of(i * 512, 512), 512)].astype(f32)
        t = t * t
        return total + ((t[:, :128] + t[:, 128:256]) + (t[:, 256:384] + t[:, 384:]))

    total = lax.fori_loop(0, 16, square, jnp.zeros((128, 128), f32))
    inv = lax.rsqrt(jnp.sum(total, axis=1, keepdims=True) * (1.0 / 8192) + 1e-05)
    inv_ref[...] = inv

    arrived(w_one)
    w_two = []
    for k in (1, 15):
        part = W.at[xh, y, c, :, :, b, xl]
        w_two.append(send(part, part, at(z_=zoff(k))))
    for h, k in ((0, 2), (1, 14)):
        part = W.at[xh, y, c, h, :, b, xl]
        w_two.append(send(part, part, at(z_=zoff(k))))

    def norm(s, _):
        t = tok_ref[:, pl.ds(pl.multiple_of(s * 512, 512), 512)].astype(f32)
        t = ((t * inv) * gain_ref[:, pl.ds(pl.multiple_of(s * 512, 512), 512)]).astype(bf16)
        for q in range(4):
            N[s // 8, (s // 2) % 4, s % 2, q // 2, q % 2] = t[:, 128 * q : 128 * q + 128]
        return 0

    lax.fori_loop(0, 16, norm, 0)

    n_a, n_b = [], []
    for k in range(4):
        for m in range(2):
            if (k, m) != (0, 0):
                y_, x_, c_ = (y + k) % 4, (x + k) % 4, (c + m) % 2
                n_a.append(send(N.at[:, y_, c_, 0], RA.at[:, :, ja], at(y_=y_, c_=c_)))
                n_b.append(send(N.at[x_ // 2, :, c_, 1, x_ % 2], RB.at[:, jb], at(x_=x_, c_=c_)))
    for h_ in range(2):
        for l_ in range(2):
            RA[h_, l_, ja] = N[h_, y, c, 0, l_]
    for y_ in range(4):
        RB[y_, jb] = N[xh, y_, c, 1, xl]

    arrived(w_two)
    w_a, w_b = [], []
    for k in (1, 3, 2):
        part = W.at[xh, y, c, 0, :, :, xl]
        w_a.append(send(part, part, at(y_=(y + k) % 4)))
        part = W.at[xh, y, c, 1, :, :, xl]
        w_b.append(send(part, part, at(x_=(x + k) % 4)))

    place = lax.broadcasted_iota(jnp.int32, (1024, 512), 0)
    PM[...] = jnp.where(place == pos_ref[...], 1.0, 0.0).astype(bf16)

    def over(lhs, rhs):
        return lax.dot_general(lhs, rhs, (((0,), (0,)), ((), ())), preferred_element_type=f32)

    arrived(g_a)
    arrived(n_a)

    def part_a(i, _):
        QA[i] = over(GA[...].reshape(1024, 512), RA[i // 2, i % 2].reshape(1024, 128)).astype(bf16)
        return 0

    lax.fori_loop(0, 4, part_a, 0)
    q_a = [send(QA.at[(x + k) % 4], RQA.at[k - 1], at(x_=(x + k) % 4)) for k in (1, 2, 3)]
    arrived(g_b)
    arrived(n_b)

    def part_b(i, _):
        QB[i] = over(GB[...].reshape(1024, 512), RB[i].reshape(1024, 128)).astype(bf16)
        return 0

    lax.fori_loop(0, 4, part_b, 0)
    q_b = [send(QB.at[(y + k) % 4], RQB.at[k - 1], at(y_=(y + k) % 4)) for k in (1, 2, 3)]

    arrived(w_a)
    arrived(w_b)
    sib = at(c_=1 - c)
    part_x = W.at[xh, :, c, 0, :, :, xl]
    part_y = W.at[:, y, c, 1]
    w_x = [send(part_x, part_x, at(x_=(x + k) % 4)) for k in (1, 3, 2)]
    w_y = [send(part_y, part_y, at(y_=(y + k) % 4)) for k in (1, 3, 2)]
    w_s = [send(part_x, part_x, sib), send(part_y, part_y, sib)]

    arrived(q_a)
    arrived(q_b)
    sum_a = QA[x].astype(f32)
    sum_b = QB[y].astype(f32)
    for k in range(3):
        sum_a = sum_a + RQA[k].astype(f32)
        sum_b = sum_b + RQB[k].astype(f32)
    plane = jnp.concatenate([sum_a, sum_b], axis=1).astype(bf16)
    for i in range(4):
        ZS[i] = jnp.dot(PM[256 * i : 256 * i + 256], plane, preferred_element_type=f32).astype(bf16)
    z_one = []
    for k, slot in ((1, 0), (15, 1)):
        z_one.append(send(ZS.at[(b + k) % 4], RZ.at[slot], at(z_=zoff(k))))
    for r, k in ((0, 2), (1, 14)):
        z_one.append(
            send(ZS.at[(b + 2) % 4, pl.ds(128 * r, 128)], RZ.at[2, pl.ds(128 * r, 128)], at(z_=zoff(k)))
        )
    arrived(z_one)
    group = ZS[b].astype(f32)
    for k in range(3):
        group = group + RZ[k].astype(f32)
    group = group.astype(bf16)
    for i in range(4):
        for l_ in range(2):
            C[i, l_] = group[64 * i + 32 * l_ : 64 * i + 32 * l_ + 32]
    z_two = []
    for k in range(4):
        for m in range(2):
            if (k, m) != (0, 0):
                x_ = xn if m else x
                z_two.append(send(C.at[(a + k) % 4, x_ % 2], RZ2.at[a, xl], at(z_=aoff(k), x_=x_)))
    RZ2[a, xl] = C[a, xl]

    for k, copy in zip((1, 3, 2), w_x):
        copy.wait_recv()
        x_ = (x + 4 - k) % 4
        part = W.at[x_ // 2, :, c, 0, :, :, x_ % 2]
        w_s.append(send(part, part, sib))
    for k, copy in zip((1, 3, 2), w_y):
        copy.wait_recv()
        part = W.at[:, (y + 4 - k) % 4, c, 1]
        w_s.append(send(part, part, sib))

    arrived(z_two)
    for l_ in range(2):
        own = RZ2[0, l_].astype(f32)
        for i in range(1, 4):
            own = own + RZ2[i, l_].astype(f32)
        for h in range(2):
            sg_ref[:, 256 * h + 128 * l_ : 256 * h + 128 * l_ + 128] = own[:, 128 * h : 128 * h + 128] * (1.0 / 65536)

    arrived(w_s)
    vacc[...] = jnp.zeros_like(vacc)
    racc[...] = jnp.zeros_like(racc)

    def block(s, _):
        s_ = (s // 8, (s // 2) % 4, s % 2)
        for h in range(2):
            cols = pl.ds(pl.multiple_of(s * 512 + h * 256, 256), 256)
            w = W[s_[0], s_[1], s_[2], h].reshape(512, 256)
            n = jnp.concatenate([N[s_[0], s_[1], s_[2], h, 0], N[s_[0], s_[1], s_[2], h, 1]], axis=1)
            vacc[...] += lax.dot_general(n, w, (((1,), (1,)), ((), ())), preferred_element_type=f32)
            g = jnp.dot(gv_ref[...], w, preferred_element_type=f32).astype(bf16)
            gn_ref[:, cols] = g
            r = (gain_ref[:, cols] * g.astype(f32)) * (tok_ref[:, cols].astype(f32) * inv)
            racc[...] += r[:, :128] + r[:, 128:]
        return 0

    lax.fori_loop(0, 16, block, 0)
    val_ref[...] = vacc[...].astype(bf16)
    mean_ref[...] = jnp.sum(racc[...], axis=1, keepdims=True) * (1.0 / 8192)

    for copy in sent:
        copy.wait_send()


N_COPIES = 3 + 14 + 4 + 14 + 6 + 6 + 8 + 4 + 7 + 6


def on_device(tokens, gain, w_t, grad_values, owner, master, moment1, moment2):
    idx = jnp.arange(512, dtype=jnp.int32)
    before = (owner[:, None] == owner[None, :]) & (idx[:, None] < idx[None, :])
    slot = jnp.sum(before.astype(jnp.int32), axis=0)
    pos = ((owner >> 1) & 3) * 256 + (owner >> 3) * 64 + (owner & 1) * 32 + slot

    vmem = pl.BlockSpec(memory_space=pltpu.VMEM)
    values, grad_normed, inv_rms, mean, slot_grad = pl.pallas_call(
        kernel,
        out_shape=(
            jax.ShapeDtypeStruct((128, 512), bf16),
            jax.ShapeDtypeStruct((128, 8192), bf16),
            jax.ShapeDtypeStruct((128, 1), f32),
            jax.ShapeDtypeStruct((128, 1), f32),
            jax.ShapeDtypeStruct((32, 512), f32),
        ),
        in_specs=[vmem] * 5,
        out_specs=(vmem,) * 5,
        scratch_shapes=[
            pltpu.VMEM((2, 4, 2, 2, 4, 4, 2, 16, 256), bf16),
            pltpu.VMEM((2, 4, 2, 2, 2, 128, 128), bf16),
            pltpu.VMEM((8, 128, 512), bf16),
            pltpu.VMEM((8, 128, 512), bf16),
            pltpu.VMEM((2, 2, 8, 128, 128), bf16),
            pltpu.VMEM((4, 8, 128, 128), bf16),
            pltpu.VMEM((4, 512, 128), bf16),
            pltpu.VMEM((4, 512, 128), bf16),
            pltpu.VMEM((3, 512, 128), bf16),
            pltpu.VMEM((3, 512, 128), bf16),
            pltpu.VMEM((1024, 512), bf16),
            pltpu.VMEM((4, 256, 256), bf16),
            pltpu.VMEM((3, 256, 256), bf16),
            pltpu.VMEM((4, 2, 32, 256), bf16),
            pltpu.VMEM((4, 2, 32, 256), bf16),
            pltpu.VMEM((128, 512), f32),
            pltpu.VMEM((128, 128), f32),
            pltpu.SemaphoreType.DMA((N_COPIES,)),
            pltpu.SemaphoreType.DMA((N_COPIES,)),
        ],
        compiler_params=pltpu.CompilerParams(
            collective_id=0, has_side_effects=True, vmem_limit_bytes=48 * 1024 * 1024
        ),
    )(tokens[0], gain[None], w_t, grad_values[0], pos[None])

    scaled = tokens[0].astype(f32) * inv_rms
    weighted = gain[None] * grad_normed.astype(f32)
    grad_x = (inv_rms * (weighted - scaled * mean)).astype(bf16)

    count = jnp.sum((owner == lax.axis_index("dp")).astype(jnp.int32))
    occupied = (jnp.arange(32, dtype=jnp.int32)[:, None] < count).astype(f32)
    new_moment1 = (beta_one * moment1[0] + (1.0 - beta_one) * slot_grad) * occupied
    new_moment2 = (beta_two * moment2[0] + (1.0 - beta_two) * slot_grad * slot_grad) * occupied
    step_dir = new_moment1 / bias_one / (jnp.sqrt(new_moment2 / bias_two) + adam_eps)
    new_master = (master[0] - learn_rate * step_dir) * occupied
    return (values[None], grad_x[None], new_master[None], new_moment1[None], new_moment2[None])


def solution(mesh):
    placed = (
        P("dp", "seq", None),
        P(),
        P("dp", "seq"),
        P("dp", "seq", None),
        P(),
        P("dp", None, "seq"),
        P("dp", None, "seq"),
        P("dp", None, "seq"),
    )
    return jax.shard_map(
        on_device,
        mesh=mesh,
        in_specs=placed,
        out_specs=(
            P("dp", "seq", None),
            P("dp", "seq", None),
            P("dp", None, "seq"),
            P("dp", None, "seq"),
            P("dp", None, "seq"),
        ),
        check_vma=False,
    )
```

```python
import jax
import jax.numpy as jnp
from jax import lax
from jax.experimental import pallas as pl
from jax.experimental.pallas import tpu as pltpu
from jax.sharding import PartitionSpec as P

beta_one = 0.9
beta_two = 0.95
learn_rate = 0.001
adam_eps = 1e-08
bias_one = 1.0 - 0.9**10
bias_two = 1.0 - 0.95**10

MESH = pl.DeviceIdType.MESH
f32, bf16 = jnp.float32, jnp.bfloat16


def kernel(
    tok_hbm, gain_hbm, w_hbm, gv_hbm, own_hbm,
    val_ref, GN, tok_ref, inv_ref, mean_ref, sg_ref, occ_ref,
    gain_ref, gv_ref, own_ref, W, N, NS, GA, GB, RA, RB, QA, QB, RQA, RQB, PM, ZS, RZ, C, RZ2, GT, vacc, VS,
    lsem, ssem, rsem,
):
    dp, seq = lax.axis_index("dp"), lax.axis_index("seq")
    z, xl = dp // 2, dp % 2
    xh, y, c = seq // 8, (seq // 2) % 4, seq % 2
    x = 2 * xh + xl
    a, b = z // 4, z % 4

    def at(z_=None, x_=None, y_=None, c_=None):
        z_ = z if z_ is None else z_
        x_ = x if x_ is None else x_
        y_ = y if y_ is None else y_
        c_ = c if c_ is None else c_
        return (2 * z_ + x_ % 2, 8 * (x_ // 2) + 2 * y_ + c_)

    def zoff(k):
        return (z + k) % 16

    def aoff(k):
        return 4 * ((a + k) % 4) + b

    def yoff(k):
        return (y + k) % 4

    def xoff(k):
        return (x + k) % 4

    xn = x + 1 - 2 * xl
    sib = at(c_=1 - c)

    loads = [
        pltpu.make_async_copy(w_hbm.at[:, pl.ds(256 * h, 256)], W.at[xh, y, c, h, a, b, xl], lsem.at[h])
        for h in range(2)
    ]
    loads += [pltpu.make_async_copy(gv_hbm, gv_ref, lsem.at[2])]
    loads += [pltpu.make_async_copy(gain_hbm, gain_ref, lsem.at[3])]
    loads += [
        pltpu.make_async_copy(
            tok_hbm.at[:, pl.ds(2048 * i, 2048)], tok_ref.at[:, pl.ds(2048 * i, 2048)], lsem.at[4 + i]
        )
        for i in range(4)
    ]
    loads += [pltpu.make_async_copy(own_hbm, own_ref, lsem.at[8])]
    for load in loads:
        load.start()

    barrier = pltpu.get_barrier_semaphore()
    peers = [at(z_=zoff(k)) for k in (1, 15, 2, 14, 4, 8, 12)]
    peers += [at(z_=aoff(k), x_=xn) for k in (1, 2, 3)]
    peers += [at(y_=yoff(k), c_=(c + m) % 2) for k in range(4) for m in range(2) if (k, m) != (0, 0)]
    peers += [at(x_=xoff(k), c_=(c + m) % 2) for k in (1, 2, 3) for m in range(2)]
    for peer in peers:
        pl.semaphore_signal(barrier, inc=1, device_id=peer, device_id_type=MESH)

    sent = []

    def send(src, dst, to):
        k = len(sent)
        copy = pltpu.make_async_remote_copy(
            src_ref=src, dst_ref=dst, send_sem=ssem.at[k], recv_sem=rsem.at[k],
            device_id=to, device_id_type=MESH,
        )
        copy.start()
        sent.append(copy)
        return copy

    def share(part, to):
        return send(part, part, to)

    def arrived(copies):
        for copy in copies:
            copy.wait_recv()

    def square(i, total):
        t = tok_ref[:, pl.ds(pl.multiple_of(i * 512, 512), 512)].astype(f32)
        t = t * t
        return total + ((t[:, :128] + t[:, 128:256]) + (t[:, 256:384] + t[:, 384:]))

    total = jnp.zeros((128, 128), f32)
    for i in range(4):
        loads[4 + i].wait()
        total = lax.fori_loop(4 * i, 4 * i + 4, square, total)
    inv = lax.rsqrt(jnp.sum(total, axis=1, keepdims=True) * (1.0 / 8192) + 1e-05)
    for load in loads[:4]:
        load.wait()

    def norm(s, _):
        cols = pl.ds(pl.multiple_of(s * 512, 512), 512)
        t = ((tok_ref[:, cols].astype(f32) * inv) * gain_ref[:, cols]).astype(bf16)
        for q in range(4):
            N[s // 8, (s // 2) % 4, s % 2, q // 2, q % 2] = t[:, 128 * q : 128 * q + 128]
        return 0

    lax.fori_loop(0, 16, norm, 0)

    pl.semaphore_wait(barrier, len(peers))

    w_one = [share(W.at[xh, y, c, :, a, b, xl], at(z_=aoff(k))) for k in (1, 3, 2)]

    g_a, g_b = [], []
    for k in (1, 3, 2):
        g_a.append(send(gv_ref, GA.at[y, c], at(y_=yoff(k))))
        g_b.append(send(gv_ref, GB.at[x, c], at(x_=xoff(k))))
    GA[y, c] = gv_ref[...]
    GB[x, c] = gv_ref[...]

    n_a, n_b = [], []
    for k in (1, 3, 2, 0):
        for m in range(2):
            if (k, m) != (0, 0):
                y_, x_, c_ = yoff(k), xoff(k), (c + m) % 2
                n_a.append(send(N.at[:, y_, c_, 0], RA.at[:, :, y, c], at(y_=y_, c_=c_)))
                n_b.append(send(N.at[x_ // 2, :, c_, 1, x_ % 2], RB.at[:, x, c], at(x_=x_, c_=c_)))
    n_s = send(N.at[:, :, 1 - c], NS, sib)
    for h_ in range(2):
        for l_ in range(2):
            RA[h_, l_, y, c] = N[h_, y, c, 0, l_]
    for y_ in range(4):
        RB[y_, x, c] = N[xh, y_, c, 1, xl]

    arrived(w_one)
    w_two = [share(W.at[xh, y, c, :, :, b, xl], at(z_=zoff(k))) for k in (1, 15)]
    w_two += [share(W.at[xh, y, c, h, :, b, xl], at(z_=zoff(k))) for h, k in ((0, 2), (1, 14))]

    loads[8].wait()
    row = own_ref[...]
    col = jnp.transpose(jnp.broadcast_to(row.astype(f32), (8, 512)))[:, :1].astype(jnp.int32)
    first = lax.broadcasted_iota(jnp.int32, (512, 512), 0)
    second = lax.broadcasted_iota(jnp.int32, (512, 512), 1)
    before = jnp.where((col == row) & (first < second), 1.0, 0.0)
    rank = jnp.sum(before, axis=0, keepdims=True).astype(jnp.int32)
    pos = ((row >> 1) & 3) * 256 + (row >> 3) * 64 + (row & 1) * 32 + rank
    place = lax.broadcasted_iota(jnp.int32, (1024, 512), 0)
    PM[...] = jnp.where(place == pos, 1.0, 0.0).astype(bf16)
    count = jnp.sum(jnp.where(row == dp, 1.0, 0.0), axis=1, keepdims=True)
    slot = lax.broadcasted_iota(jnp.int32, (32, 128), 0).astype(f32)
    occ_ref[...] = jnp.where(slot < count, 1.0, 0.0)

    arrived(g_a + g_b)
    g_s = [share(GA.at[:, c], sib), share(GB.at[:, c], sib)]

    arrived(w_two)
    w_a, w_b = [], []
    for k in (1, 3, 2):
        w_a.append(share(W.at[xh, y, c, 0, :, :, xl], at(y_=yoff(k))))
        w_b.append(share(W.at[xh, y, c, 1, :, :, xl], at(x_=xoff(k))))

    def over(lhs, rhs):
        return lax.dot_general(lhs, rhs, (((0,), (0,)), ((), ())), preferred_element_type=f32)

    arrived(n_a + g_s)

    def part_a(i, _):
        QA[i] = over(GA[...].reshape(1024, 512), RA[i // 2, i % 2].reshape(1024, 128)).astype(bf16)
        return 0

    lax.fori_loop(0, 4, part_a, 0)
    q_a = [send(QA.at[xoff(k)], RQA.at[k - 1], at(x_=xoff(k))) for k in (1, 3, 2)]
    arrived(n_b)

    def part_b(i, _):
        QB[i] = over(GB[...].reshape(1024, 512), RB[i].reshape(1024, 128)).astype(bf16)
        return 0

    lax.fori_loop(0, 4, part_b, 0)
    q_b = [send(QB.at[yoff(k)], RQB.at[k - 1], at(y_=yoff(k))) for k in (1, 3, 2)]

    arrived(w_a + w_b)

    def part(kind, q, k):
        if kind == "a":
            x_ = xoff(k)
            return W.at[x_ // 2, q, c, 0, :, :, x_ % 2]
        return W.at[q // 2, yoff(k), c, 1, pl.ds(2 * (q % 2), 2)]

    def to(kind, k):
        return at(x_=xoff(k)) if kind == "a" else at(y_=yoff(k))

    steps = [(kind, q) for q in range(4) for kind in "ba"]
    near = {}

    def send_near(t):
        if t < len(steps):
            kind, q = steps[t]
            near[kind, q] = [share(part(kind, q, 0), to(kind, k)) for k in (1, 3)]

    for t in range(WINDOW):
        send_near(t)

    arrived(q_a + q_b)
    sum_a = QA[x].astype(f32)
    sum_b = QB[y].astype(f32)
    for k in range(3):
        sum_a = sum_a + RQA[k].astype(f32)
        sum_b = sum_b + RQB[k].astype(f32)
    plane = jnp.concatenate([sum_a, sum_b], axis=1).astype(bf16)
    for i in range(4):
        ZS[i] = jnp.dot(PM[256 * i : 256 * i + 256], plane, preferred_element_type=f32).astype(bf16)
    z_one = []
    for k, to_slot in ((1, 0), (15, 1)):
        z_one.append(send(ZS.at[(b + k) % 4], RZ.at[to_slot], at(z_=zoff(k))))
    for r, k in ((0, 2), (1, 14)):
        half = pl.ds(128 * r, 128)
        z_one.append(send(ZS.at[(b + 2) % 4, half], RZ.at[2, half], at(z_=zoff(k))))

    z_two = []

    def over_z_one():
        arrived(z_one)
        group = ZS[b].astype(f32)
        for k in range(3):
            group = group + RZ[k].astype(f32)
        group = group.astype(bf16)
        for i in range(4):
            for l_ in range(2):
                C[i, l_] = group[64 * i + 32 * l_ : 64 * i + 32 * l_ + 32]
        for k in range(4):
            for m in range(2):
                if (k, m) != (0, 0):
                    x_ = xn if m else x
                    z_two.append(send(C.at[(a + k) % 4, x_ % 2], RZ2.at[a, xl], at(z_=aoff(k), x_=x_)))
        RZ2[a, xl] = C[a, xl]

    def over_z_two():
        arrived(z_two)
        for l_ in range(2):
            own = RZ2[0, l_].astype(f32)
            for i in range(1, 4):
                own = own + RZ2[i, l_].astype(f32)
            for h in range(2):
                lanes = slice(256 * h + 128 * l_, 256 * h + 128 * l_ + 128)
                sg_ref[:, lanes] = own[:, 128 * h : 128 * h + 128] * (1.0 / 65536)

    arrived([n_s])
    vacc[...] = jnp.zeros_like(vacc)

    def block(x_, y_, h):
        w = W[x_, y_, c, h].reshape(512, 256)
        n = jnp.concatenate([N[x_, y_, c, h, 0], N[x_, y_, c, h, 1]], axis=1)
        m = jnp.concatenate([NS[x_, y_, h, 0], NS[x_, y_, h, 1]], axis=1)
        n = jnp.concatenate([n, m], axis=0)
        vacc[...] += lax.dot_general(n, w, (((1,), (1,)), ((), ())), preferred_element_type=f32)
        g = jnp.concatenate([gv_ref[...], GA[y, 1 - c]], axis=0)
        g = jnp.dot(g, w, preferred_element_type=f32).astype(bf16)
        GN[x_, y_, c, h] = g[:128]
        GT[x_, y_, h] = g[128:]

    back = []

    def compute(kind, q):
        if kind == "a":

            def blocks(i, _):
                block(i, q, 0)
                return 0

            lax.fori_loop(0, 2, blocks, 0)
            back.append(send(GT.at[:, q, 0], GN.at[:, q, c, 0], sib))
        elif q % 2 == 1:

            def blocks(i, _):
                block(q // 2, i, 1)
                return 0

            lax.fori_loop(0, 4, blocks, 0)
            back.append(send(GT.at[q // 2, :, 1], GN.at[q // 2, :, c, 1], sib))

    far = {}
    for t in range(len(steps) + LAG):
        if t < len(steps):
            kind, q = steps[t]
            arrived(near[kind, q])
            k = 3 if q % 2 == 0 else 1
            far[kind, q] = share(part(kind, q, k), to(kind, 4 - k))
            send_near(t + WINDOW)
        if t >= LAG:
            kind, q = steps[t - LAG]
            arrived([far[kind, q]])
            compute(kind, q)
        if t == ZA:
            over_z_one()
        if t == ZB:
            over_z_two()

    back.append(send(vacc.at[pl.ds(128, 128)], VS, sib))
    arrived(back)
    total = vacc[:128] + VS[...]
    val_ref[...] = total.astype(bf16)
    mean = jnp.sum(gv_ref[...].astype(f32) * total, axis=1, keepdims=True) * (1.0 / 8192)

    mean_ref[...] = mean
    inv_ref[...] = inv
    for copy in sent:
        copy.wait_send()


WINDOW, LAG, ZA, ZB = 6, 4, 4, 9
N_COPIES = 3 + 6 + 15 + 4 + 2 + 6 + 6 + 16 + 4 + 7 + 8 + 7


def finish(
    tok_ref, gain_ref, gn_ref, inv_ref, mean_ref, sg_ref, occ_ref, val_ref, old_ref, m1_ref, m2_ref,
    val_out, gx_out, new_ref, n1_ref, n2_ref,
    gx, sem,
):
    inv, mean = inv_ref[...], mean_ref[...]
    copies = []
    for n in range(8):
        for s in (2 * n, 2 * n + 1):
            for h in range(2):
                cols = slice(512 * s + 256 * h, 512 * s + 256 * h + 256)
                weighted = gain_ref[:, cols] * gn_ref[s // 8, (s // 2) % 4, s % 2, h].astype(f32)
                scaled = tok_ref[:, cols].astype(f32) * inv
                gx[:, cols] = (inv * (weighted - scaled * mean)).astype(bf16)
        cols = pl.ds(1024 * n, 1024)
        copies.append(pltpu.make_async_copy(gx.at[:, cols], gx_out.at[:, cols], sem.at[n]))
        copies[-1].start()
    val_out[...] = val_ref[...]
    occupied, grad = occ_ref[:, :1], sg_ref[...]
    moment1 = (beta_one * m1_ref[...] + (1.0 - beta_one) * grad) * occupied
    moment2 = (beta_two * m2_ref[...] + (1.0 - beta_two) * grad * grad) * occupied
    step_dir = moment1 / bias_one / (jnp.sqrt(moment2 / bias_two) + adam_eps)
    new_ref[...] = (old_ref[...] - learn_rate * step_dir) * occupied
    n1_ref[...] = moment1
    n2_ref[...] = moment2
    for copy in copies:
        copy.wait()


def on_device(tokens, gain, w_t, grad_values, owner, master, moment1, moment2):
    vmem = pl.BlockSpec(memory_space=pltpu.VMEM)
    hbm = pl.BlockSpec(memory_space=pltpu.HBM)

    def far(array):
        return pltpu.with_memory_space_constraint(array, pltpu.HBM)

    values, grad_normed, tok, inv_rms, mean, slot_grad, occupied = pl.pallas_call(
        kernel,
        out_shape=(
            jax.ShapeDtypeStruct((128, 512), bf16),
            jax.ShapeDtypeStruct((2, 4, 2, 2, 128, 256), bf16),
            jax.ShapeDtypeStruct((128, 8192), bf16),
            jax.ShapeDtypeStruct((128, 1), f32),
            jax.ShapeDtypeStruct((128, 1), f32),
            jax.ShapeDtypeStruct((32, 512), f32),
            jax.ShapeDtypeStruct((32, 128), f32),
        ),
        in_specs=[hbm] * 5,
        out_specs=(vmem,) * 7,
        scratch_shapes=[
            pltpu.VMEM((1, 8192), f32),
            pltpu.VMEM((128, 512), bf16),
            pltpu.VMEM((1, 512), jnp.int32),
            pltpu.VMEM((2, 4, 2, 2, 4, 4, 2, 16, 256), bf16),
            pltpu.VMEM((2, 4, 2, 2, 2, 128, 128), bf16),
            pltpu.VMEM((2, 4, 2, 2, 128, 128), bf16),
            pltpu.VMEM((4, 2, 128, 512), bf16),
            pltpu.VMEM((4, 2, 128, 512), bf16),
            pltpu.VMEM((2, 2, 4, 2, 128, 128), bf16),
            pltpu.VMEM((4, 4, 2, 128, 128), bf16),
            pltpu.VMEM((4, 512, 128), bf16),
            pltpu.VMEM((4, 512, 128), bf16),
            pltpu.VMEM((3, 512, 128), bf16),
            pltpu.VMEM((3, 512, 128), bf16),
            pltpu.VMEM((1024, 512), bf16),
            pltpu.VMEM((4, 256, 256), bf16),
            pltpu.VMEM((3, 256, 256), bf16),
            pltpu.VMEM((4, 2, 32, 256), bf16),
            pltpu.VMEM((4, 2, 32, 256), bf16),
            pltpu.VMEM((2, 4, 2, 128, 256), bf16),
            pltpu.VMEM((256, 512), f32),
            pltpu.VMEM((128, 512), f32),
            pltpu.SemaphoreType.DMA((9,)),
            pltpu.SemaphoreType.DMA((N_COPIES,)),
            pltpu.SemaphoreType.DMA((N_COPIES,)),
        ],
        compiler_params=pltpu.CompilerParams(
            collective_id=0, has_side_effects=True, vmem_limit_bytes=40 * 1024 * 1024
        ),
    )(far(tokens[0]), far(gain[None]), far(w_t), far(grad_values[0]), far(owner[None]))

    state = jax.ShapeDtypeStruct((32, 512), f32)
    values, grad_x, new_master, new_moment1, new_moment2 = pl.pallas_call(
        finish,
        out_shape=(
            jax.ShapeDtypeStruct((128, 512), bf16),
            jax.ShapeDtypeStruct((128, 8192), bf16),
            state,
            state,
            state,
        ),
        in_specs=[vmem] * 11,
        out_specs=(vmem, hbm, vmem, vmem, vmem),
        scratch_shapes=[pltpu.VMEM((128, 8192), bf16), pltpu.SemaphoreType.DMA((8,))],
        compiler_params=pltpu.CompilerParams(vmem_limit_bytes=8 * 1024 * 1024),
    )(tok, gain[None], grad_normed, inv_rms, mean, slot_grad, occupied, values, master[0], moment1[0], moment2[0])
    return (values[None], grad_x[None], new_master[None], new_moment1[None], new_moment2[None])


def solution(mesh):
    placed = (
        P("dp", "seq", None),
        P(),
        P("dp", "seq"),
        P("dp", "seq", None),
        P(),
        P("dp", None, "seq"),
        P("dp", None, "seq"),
        P("dp", None, "seq"),
    )
    return jax.shard_map(
        on_device,
        mesh=mesh,
        in_specs=placed,
        out_specs=(
            P("dp", "seq", None),
            P("dp", "seq", None),
            P("dp", None, "seq"),
            P("dp", None, "seq"),
            P("dp", None, "seq"),
        ),
        check_vma=False,
    )
```

```python
import jax
import jax.numpy as jnp
from jax import lax
from jax.experimental import pallas as pl
from jax.experimental.pallas import tpu as pltpu
from jax.sharding import PartitionSpec as P

beta_one = 0.9
beta_two = 0.95
learn_rate = 0.001
adam_eps = 1e-08
bias_one = 1.0 - 0.9**10
bias_two = 1.0 - 0.95**10

MESH = pl.DeviceIdType.MESH
f32, bf16 = jnp.float32, jnp.bfloat16


def kernel(
    tok_hbm, gain_hbm, w_hbm, gv_hbm, own_hbm,
    val_ref, GN, tok_ref, inv_ref, mean_ref, sg_ref, occ_ref,
    gain_ref, gv_ref, own_ref, W, N, NS, GA, GB, RA, RB, QA, QB, RQA, RQB, PM, ZS, RZ, C, RZ2, GT, vacc, VS,
    lsem, ssem, rsem, far_sem,
):
    dp, seq = lax.axis_index("dp"), lax.axis_index("seq")
    z, xl = dp // 2, dp % 2
    xh, y, c = seq // 8, (seq // 2) % 4, seq % 2
    x = 2 * xh + xl
    a, b = z // 4, z % 4

    def at(z_=None, x_=None, y_=None, c_=None):
        z_ = z if z_ is None else z_
        x_ = x if x_ is None else x_
        y_ = y if y_ is None else y_
        c_ = c if c_ is None else c_
        return (2 * z_ + x_ % 2, 8 * (x_ // 2) + 2 * y_ + c_)

    def zoff(k):
        return (z + k) % 16

    def aoff(k):
        return 4 * ((a + k) % 4) + b

    def yoff(k):
        return (y + k) % 4

    def xoff(k):
        return (x + k) % 4

    xn = x + 1 - 2 * xl
    sib = at(c_=1 - c)

    loads = [
        pltpu.make_async_copy(w_hbm.at[:, pl.ds(256 * h, 256)], W.at[xh, y, c, h, a, b, xl], lsem.at[h])
        for h in range(2)
    ]
    loads += [pltpu.make_async_copy(gv_hbm, gv_ref, lsem.at[2])]
    loads += [pltpu.make_async_copy(gain_hbm, gain_ref, lsem.at[3])]
    loads += [
        pltpu.make_async_copy(
            tok_hbm.at[:, pl.ds(2048 * i, 2048)], tok_ref.at[:, pl.ds(2048 * i, 2048)], lsem.at[4 + i]
        )
        for i in range(4)
    ]
    loads += [pltpu.make_async_copy(own_hbm, own_ref, lsem.at[8])]
    for load in loads:
        load.start()

    barrier = pltpu.get_barrier_semaphore()
    peers = [at(z_=zoff(k)) for k in (4, 12, 1, 15, 2, 14)]
    peers += [at(y_=yoff(k), c_=(c + m) % 2) for k in range(4) for m in range(2) if (k, m) != (0, 0)]
    peers += [at(x_=xoff(k), c_=(c + m) % 2) for k in (1, 2, 3) for m in range(2)]
    for peer in peers:
        pl.semaphore_signal(barrier, inc=1, device_id=peer, device_id_type=MESH)

    sent = []

    def send(src, dst, to):
        k = len(sent)
        copy = pltpu.make_async_remote_copy(
            src_ref=src, dst_ref=dst, send_sem=ssem.at[k], recv_sem=rsem.at[k],
            device_id=to, device_id_type=MESH,
        )
        copy.start()
        sent.append(copy)
        return copy

    def share(part, to):
        return send(part, part, to)

    def arrived(copies):
        for copy in copies:
            copy.wait_recv()

    def square(i, total):
        t = tok_ref[:, pl.ds(pl.multiple_of(i * 512, 512), 512)].astype(f32)
        t = t * t
        return total + ((t[:, :128] + t[:, 128:256]) + (t[:, 256:384] + t[:, 384:]))

    total = jnp.zeros((128, 128), f32)
    for i in range(4):
        loads[4 + i].wait()
        total = lax.fori_loop(4 * i, 4 * i + 4, square, total)
    inv = lax.rsqrt(jnp.sum(total, axis=1, keepdims=True) * (1.0 / 8192) + 1e-05)
    for load in loads[:4] + loads[8:]:
        load.wait()

    def norm(s, _):
        cols = pl.ds(pl.multiple_of(s * 512, 512), 512)
        t = ((tok_ref[:, cols].astype(f32) * inv) * gain_ref[:, cols]).astype(bf16)
        for q in range(4):
            N[s // 8, (s // 2) % 4, s % 2, q // 2, q % 2] = t[:, 128 * q : 128 * q + 128]
        return 0

    lax.fori_loop(0, 16, norm, 0)

    pl.semaphore_wait(barrier, len(peers))

    w_one = []
    for k in (1, 3):
        pl.semaphore_signal(far_sem, inc=1, device_id=at(z_=aoff(k)), device_id_type=MESH)
        w_one.append(share(W.at[xh, y, c, :, a, b, xl], at(z_=aoff(k))))

    g_a, g_b = [], []
    for k in (1, 3, 2):
        g_a.append(send(gv_ref, GA.at[y, c], at(y_=yoff(k))))
        g_b.append(send(gv_ref, GB.at[x, c], at(x_=xoff(k))))
    pl.semaphore_wait(far_sem, 2)
    w_one.append(share(W.at[xh, y, c, :, a, b, xl], at(z_=aoff(2))))
    GA[y, c] = gv_ref[...]
    GB[x, c] = gv_ref[...]

    n_a, n_b = [], []
    for k in (1, 3, 2, 0):
        for m in range(2):
            if (k, m) != (0, 0):
                y_, x_, c_ = yoff(k), xoff(k), (c + m) % 2
                n_a.append(send(N.at[:, y_, c_, 0], RA.at[:, :, y, c], at(y_=y_, c_=c_)))
                n_b.append(send(N.at[x_ // 2, :, c_, 1, x_ % 2], RB.at[:, x, c], at(x_=x_, c_=c_)))
    n_s = send(N.at[:, :, 1 - c], NS, sib)
    for h_ in range(2):
        for l_ in range(2):
            RA[h_, l_, y, c] = N[h_, y, c, 0, l_]
    for y_ in range(4):
        RB[y_, x, c] = N[xh, y_, c, 1, xl]

    arrived(w_one)
    w_two = [share(W.at[xh, y, c, :, :, b, xl], at(z_=zoff(k))) for k in (1, 15)]
    w_two += [share(W.at[xh, y, c, h, :, b, xl], at(z_=zoff(k))) for h, k in ((0, 2), (1, 14))]

    row = own_ref[...]
    col = jnp.transpose(jnp.broadcast_to(row.astype(f32), (8, 512)))[:, :1].astype(jnp.int32)
    first = lax.broadcasted_iota(jnp.int32, (512, 512), 0)
    second = lax.broadcasted_iota(jnp.int32, (512, 512), 1)
    before = jnp.where((col == row) & (first < second), 1.0, 0.0)
    rank = jnp.sum(before, axis=0, keepdims=True).astype(jnp.int32)
    pos = ((row >> 1) & 3) * 256 + (row >> 3) * 64 + (row & 1) * 32 + rank
    place = lax.broadcasted_iota(jnp.int32, (1024, 512), 0)
    PM[...] = jnp.where(place == pos, 1.0, 0.0).astype(bf16)
    count = jnp.sum(jnp.where(row == dp, 1.0, 0.0), axis=1, keepdims=True)
    slot = lax.broadcasted_iota(jnp.int32, (32, 128), 0).astype(f32)
    occ_ref[...] = jnp.where(slot < count, 1.0, 0.0)

    arrived(g_a + g_b)
    g_s = [share(GA.at[:, c], sib), share(GB.at[:, c], sib)]

    arrived(w_two)
    w_a, w_b = [], []
    for k in (1, 3, 2):
        w_a.append(share(W.at[xh, y, c, 0, :, :, xl], at(y_=yoff(k))))
        w_b.append(share(W.at[xh, y, c, 1, :, :, xl], at(x_=xoff(k))))

    def over(lhs, rhs):
        return lax.dot_general(lhs, rhs, (((0,), (0,)), ((), ())), preferred_element_type=f32)

    arrived(n_a + g_s)

    def part_a(i, _):
        QA[i] = over(GA[...].reshape(1024, 512), RA[i // 2, i % 2].reshape(1024, 128)).astype(bf16)
        return 0

    lax.fori_loop(0, 4, part_a, 0)
    q_a = [send(QA.at[xoff(k)], RQA.at[k - 1], at(x_=xoff(k))) for k in (1, 3, 2)]
    arrived(n_b)

    def part_b(i, _):
        QB[i] = over(GB[...].reshape(1024, 512), RB[i].reshape(1024, 128)).astype(bf16)
        return 0

    lax.fori_loop(0, 4, part_b, 0)
    q_b = [send(QB.at[yoff(k)], RQB.at[k - 1], at(y_=yoff(k))) for k in (1, 3, 2)]

    arrived(w_a + w_b)

    def part(kind, q, k):
        if kind == "a":
            x_ = xoff(k)
            return W.at[x_ // 2, q, c, 0, :, :, x_ % 2]
        return W.at[q // 2, yoff(k), c, 1, pl.ds(2 * (q % 2), 2)]

    def to(kind, k):
        return at(x_=xoff(k)) if kind == "a" else at(y_=yoff(k))

    steps = [(kind, q) for q in range(4) for kind in "ba"]
    near = {}

    def send_near(t):
        if t < len(steps):
            kind, q = steps[t]
            near[kind, q] = [share(part(kind, q, 0), to(kind, k)) for k in (1, 3)]

    for t in range(WINDOW):
        send_near(t)

    arrived(q_a + q_b)
    sum_a = QA[x].astype(f32)
    sum_b = QB[y].astype(f32)
    for k in range(3):
        sum_a = sum_a + RQA[k].astype(f32)
        sum_b = sum_b + RQB[k].astype(f32)
    plane = jnp.concatenate([sum_a, sum_b], axis=1).astype(bf16)
    for i in range(4):
        ZS[i] = jnp.dot(PM[256 * i : 256 * i + 256], plane, preferred_element_type=f32).astype(bf16)
    z_one = []
    for k, to_slot in ((1, 0), (15, 1)):
        z_one.append(send(ZS.at[(b + k) % 4], RZ.at[to_slot], at(z_=zoff(k))))
    for r, k in ((0, 2), (1, 14)):
        half = pl.ds(128 * r, 128)
        z_one.append(send(ZS.at[(b + 2) % 4, half], RZ.at[2, half], at(z_=zoff(k))))

    z_two = []

    def over_z_one():
        arrived(z_one)
        group = ZS[b].astype(f32)
        for k in range(3):
            group = group + RZ[k].astype(f32)
        group = group.astype(bf16)
        for i in range(4):
            for l_ in range(2):
                C[i, l_] = group[64 * i + 32 * l_ : 64 * i + 32 * l_ + 32]
        for k in range(4):
            for m in range(2):
                if (k, m) != (0, 0):
                    x_ = xn if m else x
                    z_two.append(send(C.at[(a + k) % 4, x_ % 2], RZ2.at[a, xl], at(z_=aoff(k), x_=x_)))
        RZ2[a, xl] = C[a, xl]

    def over_z_two():
        arrived(z_two)
        for l_ in range(2):
            own = RZ2[0, l_].astype(f32)
            for i in range(1, 4):
                own = own + RZ2[i, l_].astype(f32)
            for h in range(2):
                lanes = slice(256 * h + 128 * l_, 256 * h + 128 * l_ + 128)
                sg_ref[:, lanes] = own[:, 128 * h : 128 * h + 128] * (1.0 / 65536)

    arrived([n_s])
    vacc[...] = jnp.zeros_like(vacc)

    def block(x_, y_, h):
        w = W[x_, y_, c, h].reshape(512, 256)
        n = jnp.concatenate([N[x_, y_, c, h, 0], N[x_, y_, c, h, 1]], axis=1)
        m = jnp.concatenate([NS[x_, y_, h, 0], NS[x_, y_, h, 1]], axis=1)
        n = jnp.concatenate([n, m], axis=0)
        vacc[...] += lax.dot_general(n, w, (((1,), (1,)), ((), ())), preferred_element_type=f32)
        g = jnp.concatenate([gv_ref[...], GA[y, 1 - c]], axis=0)
        g = jnp.dot(g, w, preferred_element_type=f32).astype(bf16)
        GN[x_, y_, c, h] = g[:128]
        GT[x_, y_, h] = g[128:]

    back = []

    def compute(kind, q):
        if kind == "a":

            def blocks(i, _):
                block(i, q, 0)
                return 0

            lax.fori_loop(0, 2, blocks, 0)
            back.append(send(GT.at[:, q, 0], GN.at[:, q, c, 0], sib))
        elif q % 2 == 1:

            def blocks(i, _):
                block(q // 2, i, 1)
                return 0

            lax.fori_loop(0, 4, blocks, 0)
            back.append(send(GT.at[q // 2, :, 1], GN.at[q // 2, :, c, 1], sib))

    far = {}
    for t in range(len(steps) + LAG):
        if t < len(steps):
            kind, q = steps[t]
            arrived(near[kind, q])
            k = 3 if q % 2 == 0 else 1
            far[kind, q] = share(part(kind, q, k), to(kind, 4 - k))
            send_near(t + WINDOW)
        if t >= LAG:
            kind, q = steps[t - LAG]
            arrived([far[kind, q]])
            compute(kind, q)
        if t == ZA:
            over_z_one()
        if t == ZB:
            over_z_two()

    back.append(send(vacc.at[pl.ds(128, 128)], VS, sib))
    arrived(back)
    total = vacc[:128] + VS[...]
    val_ref[...] = total.astype(bf16)
    mean = jnp.sum(gv_ref[...].astype(f32) * total, axis=1, keepdims=True) * (1.0 / 8192)

    mean_ref[...] = mean
    inv_ref[...] = inv
    for copy in sent:
        copy.wait_send()


WINDOW, LAG, ZA, ZB = 6, 6, 4, 11
N_COPIES = 3 + 6 + 15 + 4 + 2 + 6 + 6 + 16 + 4 + 7 + 8 + 7


def finish(
    tok_ref, gain_ref, gn_ref, inv_ref, mean_ref, sg_ref, occ_ref, val_ref, old_ref, m1_ref, m2_ref,
    val_out, gx_out, new_ref, n1_ref, n2_ref,
    gx, sem,
):
    inv, mean = inv_ref[...], mean_ref[...]
    copies = []
    for n in range(8):
        for s in (2 * n, 2 * n + 1):
            for h in range(2):
                cols = slice(512 * s + 256 * h, 512 * s + 256 * h + 256)
                weighted = gain_ref[:, cols] * gn_ref[s // 8, (s // 2) % 4, s % 2, h].astype(f32)
                scaled = tok_ref[:, cols].astype(f32) * inv
                gx[:, cols] = (inv * (weighted - scaled * mean)).astype(bf16)
        cols = pl.ds(1024 * n, 1024)
        copies.append(pltpu.make_async_copy(gx.at[:, cols], gx_out.at[:, cols], sem.at[n]))
        copies[-1].start()
    val_out[...] = val_ref[...]
    occupied, grad = occ_ref[:, :1], sg_ref[...]
    moment1 = (beta_one * m1_ref[...] + (1.0 - beta_one) * grad) * occupied
    moment2 = (beta_two * m2_ref[...] + (1.0 - beta_two) * grad * grad) * occupied
    step_dir = moment1 / bias_one / (jnp.sqrt(moment2 / bias_two) + adam_eps)
    new_ref[...] = (old_ref[...] - learn_rate * step_dir) * occupied
    n1_ref[...] = moment1
    n2_ref[...] = moment2
    for copy in copies:
        copy.wait()


def on_device(tokens, gain, w_t, grad_values, owner, master, moment1, moment2):
    vmem = pl.BlockSpec(memory_space=pltpu.VMEM)
    hbm = pl.BlockSpec(memory_space=pltpu.HBM)

    def far(array):
        return pltpu.with_memory_space_constraint(array, pltpu.HBM)

    values, grad_normed, tok, inv_rms, mean, slot_grad, occupied = pl.pallas_call(
        kernel,
        out_shape=(
            jax.ShapeDtypeStruct((128, 512), bf16),
            jax.ShapeDtypeStruct((2, 4, 2, 2, 128, 256), bf16),
            jax.ShapeDtypeStruct((128, 8192), bf16),
            jax.ShapeDtypeStruct((128, 1), f32),
            jax.ShapeDtypeStruct((128, 1), f32),
            jax.ShapeDtypeStruct((32, 512), f32),
            jax.ShapeDtypeStruct((32, 128), f32),
        ),
        in_specs=[hbm] * 5,
        out_specs=(vmem,) * 7,
        scratch_shapes=[
            pltpu.VMEM((1, 8192), f32),
            pltpu.VMEM((128, 512), bf16),
            pltpu.VMEM((1, 512), jnp.int32),
            pltpu.VMEM((2, 4, 2, 2, 4, 4, 2, 16, 256), bf16),
            pltpu.VMEM((2, 4, 2, 2, 2, 128, 128), bf16),
            pltpu.VMEM((2, 4, 2, 2, 128, 128), bf16),
            pltpu.VMEM((4, 2, 128, 512), bf16),
            pltpu.VMEM((4, 2, 128, 512), bf16),
            pltpu.VMEM((2, 2, 4, 2, 128, 128), bf16),
            pltpu.VMEM((4, 4, 2, 128, 128), bf16),
            pltpu.VMEM((4, 512, 128), bf16),
            pltpu.VMEM((4, 512, 128), bf16),
            pltpu.VMEM((3, 512, 128), bf16),
            pltpu.VMEM((3, 512, 128), bf16),
            pltpu.VMEM((1024, 512), bf16),
            pltpu.VMEM((4, 256, 256), bf16),
            pltpu.VMEM((3, 256, 256), bf16),
            pltpu.VMEM((4, 2, 32, 256), bf16),
            pltpu.VMEM((4, 2, 32, 256), bf16),
            pltpu.VMEM((2, 4, 2, 128, 256), bf16),
            pltpu.VMEM((256, 512), f32),
            pltpu.VMEM((128, 512), f32),
            pltpu.SemaphoreType.DMA((9,)),
            pltpu.SemaphoreType.DMA((N_COPIES,)),
            pltpu.SemaphoreType.DMA((N_COPIES,)),
            pltpu.SemaphoreType.REGULAR,
        ],
        compiler_params=pltpu.CompilerParams(
            collective_id=0, has_side_effects=True, vmem_limit_bytes=40 * 1024 * 1024
        ),
    )(far(tokens[0]), far(gain[None]), far(w_t), far(grad_values[0]), far(owner[None]))

    state = jax.ShapeDtypeStruct((32, 512), f32)
    values, grad_x, new_master, new_moment1, new_moment2 = pl.pallas_call(
        finish,
        out_shape=(
            jax.ShapeDtypeStruct((128, 512), bf16),
            jax.ShapeDtypeStruct((128, 8192), bf16),
            state,
            state,
            state,
        ),
        in_specs=[vmem] * 11,
        out_specs=(vmem, hbm, vmem, vmem, vmem),
        scratch_shapes=[pltpu.VMEM((128, 8192), bf16), pltpu.SemaphoreType.DMA((8,))],
        compiler_params=pltpu.CompilerParams(vmem_limit_bytes=8 * 1024 * 1024),
    )(tok, gain[None], grad_normed, inv_rms, mean, slot_grad, occupied, values, master[0], moment1[0], moment2[0])
    return (values[None], grad_x[None], new_master[None], new_moment1[None], new_moment2[None])


def solution(mesh):
    placed = (
        P("dp", "seq", None),
        P(),
        P("dp", "seq"),
        P("dp", "seq", None),
        P(),
        P("dp", None, "seq"),
        P("dp", None, "seq"),
        P("dp", None, "seq"),
    )
    return jax.shard_map(
        on_device,
        mesh=mesh,
        in_specs=placed,
        out_specs=(
            P("dp", "seq", None),
            P("dp", "seq", None),
            P("dp", None, "seq"),
            P("dp", None, "seq"),
            P("dp", None, "seq"),
        ),
        check_vma=False,
    )
```

```python
import jax
import jax.numpy as jnp
from jax import lax
from jax.experimental import pallas as pl
from jax.experimental.pallas import tpu as pltpu
from jax.sharding import PartitionSpec as P

beta_one = 0.9
beta_two = 0.95
learn_rate = 0.001
adam_eps = 1e-08
bias_one = 1.0 - 0.9**10
bias_two = 1.0 - 0.95**10

MESH = pl.DeviceIdType.MESH
f32, bf16 = jnp.float32, jnp.bfloat16


def kernel(
    tok_hbm, gain_hbm, w_hbm, gv_hbm, own_hbm,
    val_ref, GN, tok_ref, inv_ref, mean_ref, sg_ref, occ_ref,
    gain_ref, gv_ref, own_ref, W, N, NS, GA, GB, RA, RB, QA, QB, RQA, RQB, PM, ZS, RZ, C, RZ2, GT, vacc, VS,
    lsem, ssem, rsem, far_sem,
):
    dp, seq = lax.axis_index("dp"), lax.axis_index("seq")
    z, xl = dp // 2, dp % 2
    xh, y, c = seq // 8, (seq // 2) % 4, seq % 2
    x = 2 * xh + xl
    a, b = z // 4, z % 4

    def at(z_=None, x_=None, y_=None, c_=None):
        z_ = z if z_ is None else z_
        x_ = x if x_ is None else x_
        y_ = y if y_ is None else y_
        c_ = c if c_ is None else c_
        return (2 * z_ + x_ % 2, 8 * (x_ // 2) + 2 * y_ + c_)

    def zoff(k):
        return (z + k) % 16

    def aoff(k):
        return 4 * ((a + k) % 4) + b

    def yoff(k):
        return (y + k) % 4

    def xoff(k):
        return (x + k) % 4

    xn = x + 1 - 2 * xl
    sib = at(c_=1 - c)

    loads = [
        pltpu.make_async_copy(w_hbm.at[:, pl.ds(256 * h, 256)], W.at[xh, y, c, h, a, b, xl], lsem.at[h])
        for h in range(2)
    ]
    loads += [pltpu.make_async_copy(gv_hbm, gv_ref, lsem.at[2])]
    loads += [pltpu.make_async_copy(gain_hbm, gain_ref, lsem.at[3])]
    loads += [
        pltpu.make_async_copy(
            tok_hbm.at[:, pl.ds(2048 * i, 2048)], tok_ref.at[:, pl.ds(2048 * i, 2048)], lsem.at[4 + i]
        )
        for i in range(4)
    ]
    loads += [pltpu.make_async_copy(own_hbm, own_ref, lsem.at[8])]
    for load in loads:
        load.start()

    barrier = pltpu.get_barrier_semaphore()
    peers = [at(z_=zoff(k)) for k in (4, 12, 1, 15, 2, 14)]
    peers += [at(y_=yoff(k), c_=(c + m) % 2) for k in range(4) for m in range(2) if (k, m) != (0, 0)]
    peers += [at(x_=xoff(k), c_=(c + m) % 2) for k in (1, 2, 3) for m in range(2)]
    for peer in peers:
        pl.semaphore_signal(barrier, inc=1, device_id=peer, device_id_type=MESH)

    sent = []

    def send(src, dst, to):
        k = len(sent)
        copy = pltpu.make_async_remote_copy(
            src_ref=src, dst_ref=dst, send_sem=ssem.at[k], recv_sem=rsem.at[k],
            device_id=to, device_id_type=MESH,
        )
        copy.start()
        sent.append(copy)
        return copy

    def share(part, to):
        return send(part, part, to)

    def arrived(copies):
        for copy in copies:
            copy.wait_recv()

    def square(i, total):
        t = tok_ref[:, pl.ds(pl.multiple_of(i * 512, 512), 512)].astype(f32)
        t = t * t
        return total + ((t[:, :128] + t[:, 128:256]) + (t[:, 256:384] + t[:, 384:]))

    total = jnp.zeros((128, 128), f32)
    for i in range(4):
        loads[4 + i].wait()
        total = lax.fori_loop(4 * i, 4 * i + 4, square, total)
    inv = lax.rsqrt(jnp.sum(total, axis=1, keepdims=True) * (1.0 / 8192) + 1e-05)
    for load in loads[:4] + loads[8:]:
        load.wait()

    def norm(s, _):
        cols = pl.ds(pl.multiple_of(s * 512, 512), 512)
        t = ((tok_ref[:, cols].astype(f32) * inv) * gain_ref[:, cols]).astype(bf16)
        for q in range(4):
            N[s // 8, (s // 2) % 4, s % 2, q // 2, q % 2] = t[:, 128 * q : 128 * q + 128]
        return 0

    lax.fori_loop(0, 16, norm, 0)

    pl.semaphore_wait(barrier, len(peers))

    w_one = []
    for k in (1, 3):
        pl.semaphore_signal(far_sem, inc=1, device_id=at(z_=aoff(k)), device_id_type=MESH)
        w_one.append(share(W.at[xh, y, c, :, a, b, xl], at(z_=aoff(k))))

    g_a, g_b = [], []
    for k in (1, 3):
        g_a.append(send(gv_ref, GA.at[y, c], at(y_=yoff(k))))
        g_b.append(send(gv_ref, GB.at[x, c], at(x_=xoff(k))))
    pl.semaphore_wait(far_sem, 2)
    w_one.append(share(W.at[xh, y, c, :, a, b, xl], at(z_=aoff(2))))
    GA[y, c] = gv_ref[...]
    GB[x, c] = gv_ref[...]

    n_a, n_b = [], []
    for k in (1, 3, 2, 0):
        for m in range(2):
            if (k, m) != (0, 0):
                y_, x_, c_ = yoff(k), xoff(k), (c + m) % 2
                n_a.append(send(N.at[:, y_, c_, 0], RA.at[:, :, y, c], at(y_=y_, c_=c_)))
                n_b.append(send(N.at[x_ // 2, :, c_, 1, x_ % 2], RB.at[:, x, c], at(x_=x_, c_=c_)))
    n_s = send(N.at[:, :, 1 - c], NS, sib)
    for h_ in range(2):
        for l_ in range(2):
            RA[h_, l_, y, c] = N[h_, y, c, 0, l_]
    for y_ in range(4):
        RB[y_, x, c] = N[xh, y_, c, 1, xl]

    arrived(w_one)
    w_two = [share(W.at[xh, y, c, :, :, b, xl], at(z_=zoff(k))) for k in (1, 15)]
    w_two += [share(W.at[xh, y, c, h, :, b, xl], at(z_=zoff(k))) for h, k in ((0, 2), (1, 14))]

    row = own_ref[...]
    col = jnp.transpose(jnp.broadcast_to(row.astype(f32), (8, 512)))[:, :1].astype(jnp.int32)
    first = lax.broadcasted_iota(jnp.int32, (512, 512), 0)
    second = lax.broadcasted_iota(jnp.int32, (512, 512), 1)
    before = jnp.where((col == row) & (first < second), 1.0, 0.0)
    rank = jnp.sum(before, axis=0, keepdims=True).astype(jnp.int32)
    pos = ((row >> 1) & 3) * 256 + (row >> 3) * 64 + (row & 1) * 32 + rank
    place = lax.broadcasted_iota(jnp.int32, (1024, 512), 0)
    PM[...] = jnp.where(place == pos, 1.0, 0.0).astype(bf16)
    count = jnp.sum(jnp.where(row == dp, 1.0, 0.0), axis=1, keepdims=True)
    slot = lax.broadcasted_iota(jnp.int32, (32, 128), 0).astype(f32)
    occ_ref[...] = jnp.where(slot < count, 1.0, 0.0)

    arrived(g_a + g_b)
    g_far = []
    for n, k in ((0, 3), (1, 1)):
        half = pl.ds(64 * n, 64)
        g_far.append(share(GA.at[yoff(k), c, half], at(y_=yoff(4 - k))))
        g_far.append(share(GB.at[xoff(k), c, half], at(x_=xoff(4 - k))))

    def part(kind, r, k):
        x_, y_, h = (xoff(k), yoff(r), 0) if kind == "a" else (xoff(r), yoff(k), 1)
        return W.at[x_ // 2, y_, c, h, :, :, x_ % 2]

    def to(kind, k):
        return at(x_=xoff(k)) if kind == "a" else at(y_=yoff(k))

    steps = [(kind, r) for r in (0, 1, 3, 2) for kind in "ba"]
    near = {}

    def send_near(t):
        kind, r = steps[t]
        near[kind, r] = [share(part(kind, r, 0), to(kind, k)) for k in (1, 3)]

    arrived(w_two)
    w_near = []
    for k in (1, 3):
        w_near.append(share(part("a", 0, 0), at(y_=yoff(k))))
        w_near.append(share(part("b", 0, 0), at(x_=xoff(k))))
    for t in range(EARLY):
        send_near(t)
    arrived(g_far)
    g_s = [share(GA.at[:, c], sib), share(GB.at[:, c], sib)]

    def over(lhs, rhs):
        return lax.dot_general(lhs, rhs, (((0,), (0,)), ((), ())), preferred_element_type=f32)

    arrived(n_a + g_s)

    q_a, q_b = [], []
    for k in (2, 1, 3, 0):
        x_ = xoff(k)
        QA[x_] = over(RA[x_ // 2, x_ % 2].reshape(1024, 128), GA[...].reshape(1024, 512)).astype(bf16)
        if k:
            q_a.append(send(QA.at[x_], RQA.at[k - 1], at(x_=x_)))
    arrived(n_b)
    for k in (2, 1, 3, 0):
        y_ = yoff(k)
        QB[y_] = over(RB[y_].reshape(1024, 128), GB[...].reshape(1024, 512)).astype(bf16)
        if k:
            q_b.append(send(QB.at[y_], RQB.at[k - 1], at(y_=y_)))

    arrived(w_near)
    w_far = []
    for n, k in ((0, 3), (1, 1)):
        half = pl.ds(2 * n, 2)
        w_far.append(share(W.at[xh, yoff(k), c, 0, half, :, xl], at(y_=yoff(4 - k))))
        x_ = xoff(k)
        w_far.append(share(W.at[x_ // 2, y, c, 1, half, :, x_ % 2], at(x_=xoff(4 - k))))
    for t in range(EARLY, 6):
        send_near(t)

    arrived(q_a + q_b)
    sum_a = QA[x].astype(f32)
    sum_b = QB[y].astype(f32)
    for k in range(3):
        sum_a = sum_a + RQA[k].astype(f32)
        sum_b = sum_b + RQB[k].astype(f32)
    plane = jnp.concatenate([sum_a, sum_b], axis=0).astype(bf16)
    for i in range(4):
        rows = PM[256 * i : 256 * i + 256]
        ZS[i] = lax.dot_general(rows, plane, (((1,), (1,)), ((), ())), preferred_element_type=f32).astype(bf16)
    z_one = []
    for k, to_slot in ((1, 0), (15, 1)):
        z_one.append(send(ZS.at[(b + k) % 4], RZ.at[to_slot], at(z_=zoff(k))))
    for r, k in ((0, 2), (1, 14)):
        half = pl.ds(128 * r, 128)
        z_one.append(send(ZS.at[(b + 2) % 4, half], RZ.at[2, half], at(z_=zoff(k))))

    z_two = []

    def over_z_one():
        arrived(z_one)
        group = ZS[b].astype(f32)
        for k in range(3):
            group = group + RZ[k].astype(f32)
        group = group.astype(bf16)
        for i in range(4):
            for l_ in range(2):
                C[i, l_] = group[64 * i + 32 * l_ : 64 * i + 32 * l_ + 32]
        for k in range(4):
            for m in range(2):
                if (k, m) != (0, 0):
                    x_ = xn if m else x
                    z_two.append(send(C.at[(a + k) % 4, x_ % 2], RZ2.at[a, xl], at(z_=aoff(k), x_=x_)))
        RZ2[a, xl] = C[a, xl]

    def over_z_two():
        arrived(z_two)
        for l_ in range(2):
            own = RZ2[0, l_].astype(f32)
            for i in range(1, 4):
                own = own + RZ2[i, l_].astype(f32)
            for h in range(2):
                lanes = slice(256 * h + 128 * l_, 256 * h + 128 * l_ + 128)
                sg_ref[:, lanes] = own[:, 128 * h : 128 * h + 128] * (1.0 / 65536)

    arrived([n_s])
    vacc[...] = jnp.zeros_like(vacc)

    def block(x_, y_, h):
        w = W[x_, y_, c, h].reshape(512, 256)
        n = jnp.concatenate([N[x_, y_, c, h, 0], N[x_, y_, c, h, 1]], axis=1)
        m = jnp.concatenate([NS[x_, y_, h, 0], NS[x_, y_, h, 1]], axis=1)
        n = jnp.concatenate([n, m], axis=0)
        vacc[...] += lax.dot_general(n, w, (((1,), (1,)), ((), ())), preferred_element_type=f32)
        g = jnp.concatenate([gv_ref[...], GA[y, 1 - c]], axis=0)
        g = jnp.dot(g, w, preferred_element_type=f32).astype(bf16)
        GN[x_, y_, c, h] = g[:128]
        GT[x_, y_, h] = g[128:]

    back = []

    def compute(kind, r):
        if kind == "a":
            y_ = yoff(r)

            def blocks(i, _):
                block(i, y_, 0)
                return 0

            lax.fori_loop(0, 2, blocks, 0)
            back.append(send(GT.at[:, y_, 0], GN.at[:, y_, c, 0], sib))
        elif r >= 2:
            x_ = xh if r == 3 else 1 - xh

            def blocks(i, _):
                block(x_, i, 1)
                return 0

            lax.fori_loop(0, 4, blocks, 0)
            back.append(send(GT.at[x_, :, 1], GN.at[x_, :, c, 1], sib))

    far = {}
    for t in range(len(steps) + LAG):
        if t < len(steps):
            kind, r = steps[t]
            arrived(near[kind, r])
            k = 3 if r in (0, 3) else 1
            far[kind, r] = share(part(kind, r, k), to(kind, 4 - k))
        if t == WINDOW:
            arrived(w_far)
            send_near(6)
            send_near(7)
        if t >= LAG:
            kind, r = steps[t - LAG]
            arrived([far[kind, r]])
            compute(kind, r)
        if t == ZA:
            over_z_one()
        if t == ZB:
            over_z_two()

    back.append(send(vacc.at[pl.ds(128, 128)], VS, sib))
    arrived(back)
    total = vacc[:128] + VS[...]
    val_ref[...] = total.astype(bf16)
    mean = jnp.sum(gv_ref[...].astype(f32) * total, axis=1, keepdims=True) * (1.0 / 8192)

    mean_ref[...] = mean
    inv_ref[...] = inv
    for copy in sent:
        copy.wait_send()


WINDOW, LAG, ZA, ZB, EARLY = 1, 5, 3, 11, 2
N_COPIES = 3 + 8 + 15 + 4 + 2 + 8 + 6 + 16 + 4 + 7 + 8 + 7


def finish(
    tok_ref, gain_ref, gn_ref, inv_ref, mean_ref, sg_ref, occ_ref, val_ref, old_ref, m1_ref, m2_ref,
    val_out, gx_out, new_ref, n1_ref, n2_ref,
    gx, sem,
):
    inv, mean = inv_ref[...], mean_ref[...]
    copies = []
    for n in range(8):
        for s in (2 * n, 2 * n + 1):
            for h in range(2):
                cols = slice(512 * s + 256 * h, 512 * s + 256 * h + 256)
                weighted = gain_ref[:, cols] * gn_ref[s // 8, (s // 2) % 4, s % 2, h].astype(f32)
                scaled = tok_ref[:, cols].astype(f32) * inv
                gx[:, cols] = (inv * (weighted - scaled * mean)).astype(bf16)
        cols = pl.ds(1024 * n, 1024)
        copies.append(pltpu.make_async_copy(gx.at[:, cols], gx_out.at[:, cols], sem.at[n]))
        copies[-1].start()
    val_out[...] = val_ref[...]
    occupied, grad = occ_ref[:, :1], sg_ref[...]
    moment1 = (beta_one * m1_ref[...] + (1.0 - beta_one) * grad) * occupied
    moment2 = (beta_two * m2_ref[...] + (1.0 - beta_two) * grad * grad) * occupied
    step_dir = moment1 / bias_one / (jnp.sqrt(moment2 / bias_two) + adam_eps)
    new_ref[...] = (old_ref[...] - learn_rate * step_dir) * occupied
    n1_ref[...] = moment1
    n2_ref[...] = moment2
    for copy in copies:
        copy.wait()


def on_device(tokens, gain, w_t, grad_values, owner, master, moment1, moment2):
    vmem = pl.BlockSpec(memory_space=pltpu.VMEM)
    hbm = pl.BlockSpec(memory_space=pltpu.HBM)

    def far(array):
        return pltpu.with_memory_space_constraint(array, pltpu.HBM)

    values, grad_normed, tok, inv_rms, mean, slot_grad, occupied = pl.pallas_call(
        kernel,
        out_shape=(
            jax.ShapeDtypeStruct((128, 512), bf16),
            jax.ShapeDtypeStruct((2, 4, 2, 2, 128, 256), bf16),
            jax.ShapeDtypeStruct((128, 8192), bf16),
            jax.ShapeDtypeStruct((128, 1), f32),
            jax.ShapeDtypeStruct((128, 1), f32),
            jax.ShapeDtypeStruct((32, 512), f32),
            jax.ShapeDtypeStruct((32, 128), f32),
        ),
        in_specs=[hbm] * 5,
        out_specs=(vmem,) * 7,
        scratch_shapes=[
            pltpu.VMEM((1, 8192), f32),
            pltpu.VMEM((128, 512), bf16),
            pltpu.VMEM((1, 512), jnp.int32),
            pltpu.VMEM((2, 4, 2, 2, 4, 4, 2, 16, 256), bf16),
            pltpu.VMEM((2, 4, 2, 2, 2, 128, 128), bf16),
            pltpu.VMEM((2, 4, 2, 2, 128, 128), bf16),
            pltpu.VMEM((4, 2, 128, 512), bf16),
            pltpu.VMEM((4, 2, 128, 512), bf16),
            pltpu.VMEM((2, 2, 4, 2, 128, 128), bf16),
            pltpu.VMEM((4, 4, 2, 128, 128), bf16),
            pltpu.VMEM((4, 128, 512), bf16),
            pltpu.VMEM((4, 128, 512), bf16),
            pltpu.VMEM((3, 128, 512), bf16),
            pltpu.VMEM((3, 128, 512), bf16),
            pltpu.VMEM((1024, 512), bf16),
            pltpu.VMEM((4, 256, 256), bf16),
            pltpu.VMEM((3, 256, 256), bf16),
            pltpu.VMEM((4, 2, 32, 256), bf16),
            pltpu.VMEM((4, 2, 32, 256), bf16),
            pltpu.VMEM((2, 4, 2, 128, 256), bf16),
            pltpu.VMEM((256, 512), f32),
            pltpu.VMEM((128, 512), f32),
            pltpu.SemaphoreType.DMA((9,)),
            pltpu.SemaphoreType.DMA((N_COPIES,)),
            pltpu.SemaphoreType.DMA((N_COPIES,)),
            pltpu.SemaphoreType.REGULAR,
        ],
        compiler_params=pltpu.CompilerParams(
            collective_id=0, has_side_effects=True, vmem_limit_bytes=40 * 1024 * 1024
        ),
    )(far(tokens[0]), far(gain[None]), far(w_t), far(grad_values[0]), far(owner[None]))

    state = jax.ShapeDtypeStruct((32, 512), f32)
    values, grad_x, new_master, new_moment1, new_moment2 = pl.pallas_call(
        finish,
        out_shape=(
            jax.ShapeDtypeStruct((128, 512), bf16),
            jax.ShapeDtypeStruct((128, 8192), bf16),
            state,
            state,
            state,
        ),
        in_specs=[vmem] * 11,
        out_specs=(vmem, hbm, vmem, vmem, vmem),
        scratch_shapes=[pltpu.VMEM((128, 8192), bf16), pltpu.SemaphoreType.DMA((8,))],
        compiler_params=pltpu.CompilerParams(vmem_limit_bytes=8 * 1024 * 1024),
    )(tok, gain[None], grad_normed, inv_rms, mean, slot_grad, occupied, values, master[0], moment1[0], moment2[0])
    return (values[None], grad_x[None], new_master[None], new_moment1[None], new_moment2[None])


def solution(mesh):
    placed = (
        P("dp", "seq", None),
        P(),
        P("dp", "seq"),
        P("dp", "seq", None),
        P(),
        P("dp", None, "seq"),
        P("dp", None, "seq"),
        P("dp", None, "seq"),
    )
    return jax.shard_map(
        on_device,
        mesh=mesh,
        in_specs=placed,
        out_specs=(
            P("dp", "seq", None),
            P("dp", "seq", None),
            P("dp", None, "seq"),
            P("dp", None, "seq"),
            P("dp", None, "seq"),
        ),
        check_vma=False,
    )
```

```python
import jax
import jax.numpy as jnp
from jax import lax
from jax.experimental import pallas as pl
from jax.experimental.pallas import tpu as pltpu
from jax.sharding import PartitionSpec as P

beta_one = 0.9
beta_two = 0.95
learn_rate = 0.001
adam_eps = 1e-08
bias_one = 1.0 - 0.9**10
bias_two = 1.0 - 0.95**10

MESH = pl.DeviceIdType.MESH
f32, bf16 = jnp.float32, jnp.bfloat16


def kernel(
    tok_hbm, gain_hbm, w_hbm, gv_hbm, own_hbm,
    val_ref, GN, tok_ref, inv_ref, mean_ref, sg_ref, occ_ref,
    gain_ref, gv_ref, own_ref, W, N, NS, GA, GB, RA, RB, QA, QB, RQA, RQB, PM, ZS, RZ, C, RZ2, GT, vacc, VS,
    lsem, ssem, rsem, far_sem,
):
    dp, seq = lax.axis_index("dp"), lax.axis_index("seq")
    z, xl = dp // 2, dp % 2
    xh, y, c = seq // 8, (seq // 2) % 4, seq % 2
    x = 2 * xh + xl
    a, b = z // 4, z % 4

    def at(z_=None, x_=None, y_=None, c_=None):
        z_ = z if z_ is None else z_
        x_ = x if x_ is None else x_
        y_ = y if y_ is None else y_
        c_ = c if c_ is None else c_
        return (2 * z_ + x_ % 2, 8 * (x_ // 2) + 2 * y_ + c_)

    def zoff(k):
        return (z + k) % 16

    def aoff(k):
        return 4 * ((a + k) % 4) + b

    def yoff(k):
        return (y + k) % 4

    def xoff(k):
        return (x + k) % 4

    xn = x + 1 - 2 * xl
    sib = at(c_=1 - c)

    loads = [
        pltpu.make_async_copy(w_hbm.at[:, pl.ds(256 * h, 256)], W.at[xh, y, c, h, a, b, xl], lsem.at[h])
        for h in range(2)
    ]
    loads += [pltpu.make_async_copy(gv_hbm, gv_ref, lsem.at[2])]
    loads += [pltpu.make_async_copy(gain_hbm, gain_ref, lsem.at[3])]
    loads += [
        pltpu.make_async_copy(
            tok_hbm.at[:, pl.ds(2048 * i, 2048)], tok_ref.at[:, pl.ds(2048 * i, 2048)], lsem.at[4 + i]
        )
        for i in range(4)
    ]
    loads += [pltpu.make_async_copy(own_hbm, own_ref, lsem.at[8])]
    for load in loads:
        load.start()

    barrier = pltpu.get_barrier_semaphore()
    peers = [at(z_=zoff(k)) for k in (4, 12, 1, 15, 2, 14)]
    peers += [at(y_=yoff(k), c_=(c + m) % 2) for k in range(4) for m in range(2) if (k, m) != (0, 0)]
    peers += [at(x_=xoff(k), c_=(c + m) % 2) for k in (1, 2, 3) for m in range(2)]
    for peer in peers:
        pl.semaphore_signal(barrier, inc=1, device_id=peer, device_id_type=MESH)

    sent = []

    def send(src, dst, to):
        k = len(sent)
        copy = pltpu.make_async_remote_copy(
            src_ref=src, dst_ref=dst, send_sem=ssem.at[k], recv_sem=rsem.at[k],
            device_id=to, device_id_type=MESH,
        )
        copy.start()
        sent.append(copy)
        return copy

    def share(part, to):
        return send(part, part, to)

    def arrived(copies):
        for copy in copies:
            copy.wait_recv()

    def square(i, total):
        t = tok_ref[:, pl.ds(pl.multiple_of(i * 512, 512), 512)].astype(f32)
        t = t * t
        return total + ((t[:, :128] + t[:, 128:256]) + (t[:, 256:384] + t[:, 384:]))

    total = jnp.zeros((128, 128), f32)
    for i in range(4):
        loads[4 + i].wait()
        total = lax.fori_loop(4 * i, 4 * i + 4, square, total)
    inv = lax.rsqrt(jnp.sum(total, axis=1, keepdims=True) * (1.0 / 8192) + 1e-05)
    for load in loads[:4] + loads[8:]:
        load.wait()

    def norm(s, _):
        cols = pl.ds(pl.multiple_of(s * 512, 512), 512)
        t = ((tok_ref[:, cols].astype(f32) * inv) * gain_ref[:, cols]).astype(bf16)
        for q in range(4):
            N[s // 8, (s // 2) % 4, s % 2, q // 2, q % 2] = t[:, 128 * q : 128 * q + 128]
        return 0

    lax.fori_loop(0, 16, norm, 0)

    pl.semaphore_wait(barrier, len(peers))

    w_one = []
    for k in (1, 3):
        pl.semaphore_signal(far_sem, inc=1, device_id=at(z_=aoff(k)), device_id_type=MESH)
        w_one.append(share(W.at[xh, y, c, :, a, b, xl], at(z_=aoff(k))))

    g_a, g_b = [], []
    for k in (1, 3, 2):
        g_a.append(send(gv_ref, GA.at[y, c], at(y_=yoff(k))))
        g_b.append(send(gv_ref, GB.at[x, c], at(x_=xoff(k))))
    pl.semaphore_wait(far_sem, 2)
    w_one.append(share(W.at[xh, y, c, :, a, b, xl], at(z_=aoff(2))))
    GA[y, c] = gv_ref[...]
    GB[x, c] = gv_ref[...]

    n_a, n_b = [], []
    for k in (1, 3, 2, 0):
        for m in range(2):
            if (k, m) != (0, 0):
                y_, x_, c_ = yoff(k), xoff(k), (c + m) % 2
                n_a.append(send(N.at[:, y_, c_, 0], RA.at[:, :, y, c], at(y_=y_, c_=c_)))
                n_b.append(send(N.at[x_ // 2, :, c_, 1, x_ % 2], RB.at[:, x, c], at(x_=x_, c_=c_)))
    n_s = send(N.at[:, :, 1 - c], NS, sib)
    for h_ in range(2):
        for l_ in range(2):
            RA[h_, l_, y, c] = N[h_, y, c, 0, l_]
    for y_ in range(4):
        RB[y_, x, c] = N[xh, y_, c, 1, xl]

    arrived(w_one)
    w_two = [share(W.at[xh, y, c, :, :, b, xl], at(z_=zoff(k))) for k in (1, 15)]
    w_two += [share(W.at[xh, y, c, h, :, b, xl], at(z_=zoff(k))) for h, k in ((0, 2), (1, 14))]

    row = own_ref[...]
    col = jnp.transpose(jnp.broadcast_to(row.astype(f32), (8, 512)))[:, :1].astype(jnp.int32)
    first = lax.broadcasted_iota(jnp.int32, (512, 512), 0)
    second = lax.broadcasted_iota(jnp.int32, (512, 512), 1)
    before = jnp.where((col == row) & (first < second), 1.0, 0.0)
    rank = jnp.sum(before, axis=0, keepdims=True).astype(jnp.int32)
    pos = ((row >> 1) & 3) * 256 + (row >> 3) * 64 + (row & 1) * 32 + rank
    place = lax.broadcasted_iota(jnp.int32, (1024, 512), 0)
    PM[...] = jnp.where(place == pos, 1.0, 0.0).astype(bf16)
    count = jnp.sum(jnp.where(row == dp, 1.0, 0.0), axis=1, keepdims=True)
    slot = lax.broadcasted_iota(jnp.int32, (32, 128), 0).astype(f32)
    occ_ref[...] = jnp.where(slot < count, 1.0, 0.0)

    arrived(g_a + g_b)
    g_s = [share(GA.at[:, c], sib), share(GB.at[:, c], sib)]

    arrived(w_two)
    w_a, w_b = [], []
    for k in (1, 3, 2):
        w_a.append(share(W.at[xh, y, c, 0, :, :, xl], at(y_=yoff(k))))
        w_b.append(share(W.at[xh, y, c, 1, :, :, xl], at(x_=xoff(k))))

    def over(lhs, rhs):
        return lax.dot_general(lhs, rhs, (((0,), (0,)), ((), ())), preferred_element_type=f32)

    arrived(n_a + g_s)

    q_a, q_b = [], []
    for k in (2, 1, 3, 0):
        x_ = xoff(k)
        QA[x_] = over(RA[x_ // 2, x_ % 2].reshape(1024, 128), GA[...].reshape(1024, 512)).astype(bf16)
        if k:
            q_a.append(send(QA.at[x_], RQA.at[k - 1], at(x_=x_)))
    arrived(n_b)
    for k in (2, 1, 3, 0):
        y_ = yoff(k)
        QB[y_] = over(RB[y_].reshape(1024, 128), GB[...].reshape(1024, 512)).astype(bf16)
        if k:
            q_b.append(send(QB.at[y_], RQB.at[k - 1], at(y_=y_)))

    arrived(w_a + w_b)

    def part(kind, q, k):
        if kind == "a":
            x_ = xoff(k)
            return W.at[x_ // 2, q, c, 0, :, :, x_ % 2]
        return W.at[q // 2, yoff(k), c, 1, pl.ds(2 * (q % 2), 2)]

    def to(kind, k):
        return at(x_=xoff(k)) if kind == "a" else at(y_=yoff(k))

    steps = [(kind, q) for q in range(4) for kind in "ba"]
    near = {}

    def send_near(t):
        if t < len(steps):
            kind, q = steps[t]
            near[kind, q] = [share(part(kind, q, 0), to(kind, k)) for k in (1, 3)]

    for t in range(WINDOW):
        send_near(t)

    arrived(q_a + q_b)
    sum_a = QA[x].astype(f32)
    sum_b = QB[y].astype(f32)
    for k in range(3):
        sum_a = sum_a + RQA[k].astype(f32)
        sum_b = sum_b + RQB[k].astype(f32)
    plane = jnp.concatenate([sum_a, sum_b], axis=0).astype(bf16)
    for i in range(4):
        rows = PM[256 * i : 256 * i + 256]
        ZS[i] = lax.dot_general(rows, plane, (((1,), (1,)), ((), ())), preferred_element_type=f32).astype(bf16)
    z_one = []
    for k, to_slot in ((1, 0), (15, 1)):
        z_one.append(send(ZS.at[(b + k) % 4], RZ.at[to_slot], at(z_=zoff(k))))
    for r, k in ((0, 2), (1, 14)):
        half = pl.ds(128 * r, 128)
        z_one.append(send(ZS.at[(b + 2) % 4, half], RZ.at[2, half], at(z_=zoff(k))))

    z_two = []

    def over_z_one():
        arrived(z_one)
        group = ZS[b].astype(f32)
        for k in range(3):
            group = group + RZ[k].astype(f32)
        group = group.astype(bf16)
        for i in range(4):
            for l_ in range(2):
                C[i, l_] = group[64 * i + 32 * l_ : 64 * i + 32 * l_ + 32]
        for k in range(4):
            for m in range(2):
                if (k, m) != (0, 0):
                    x_ = xn if m else x
                    z_two.append(send(C.at[(a + k) % 4, x_ % 2], RZ2.at[a, xl], at(z_=aoff(k), x_=x_)))
        RZ2[a, xl] = C[a, xl]

    def over_z_two():
        arrived(z_two)
        for l_ in range(2):
            own = RZ2[0, l_].astype(f32)
            for i in range(1, 4):
                own = own + RZ2[i, l_].astype(f32)
            for h in range(2):
                lanes = slice(256 * h + 128 * l_, 256 * h + 128 * l_ + 128)
                sg_ref[:, lanes] = own[:, 128 * h : 128 * h + 128] * (1.0 / 65536)

    arrived([n_s])
    vacc[...] = jnp.zeros_like(vacc)

    def block(x_, y_, h):
        w = W[x_, y_, c, h].reshape(512, 256)
        n = jnp.concatenate([N[x_, y_, c, h, 0], N[x_, y_, c, h, 1]], axis=1)
        m = jnp.concatenate([NS[x_, y_, h, 0], NS[x_, y_, h, 1]], axis=1)
        n = jnp.concatenate([n, m], axis=0)
        vacc[...] += lax.dot_general(n, w, (((1,), (1,)), ((), ())), preferred_element_type=f32)
        g = jnp.concatenate([gv_ref[...], GA[y, 1 - c]], axis=0)
        g = jnp.dot(g, w, preferred_element_type=f32).astype(bf16)
        GN[x_, y_, c, h] = g[:128]
        GT[x_, y_, h] = g[128:]

    back = []

    def compute(kind, q):
        if kind == "a":

            def blocks(i, _):
                block(i, q, 0)
                return 0

            lax.fori_loop(0, 2, blocks, 0)
            back.append(send(GT.at[:, q, 0], GN.at[:, q, c, 0], sib))
        elif q % 2 == 1:

            def blocks(i, _):
                block(q // 2, i, 1)
                return 0

            lax.fori_loop(0, 4, blocks, 0)
            back.append(send(GT.at[q // 2, :, 1], GN.at[q // 2, :, c, 1], sib))

    far = {}
    for t in range(len(steps) + LAG):
        if t < len(steps):
            kind, q = steps[t]
            arrived(near[kind, q])
            k = 3 if q % 2 == 0 else 1
            far[kind, q] = share(part(kind, q, k), to(kind, 4 - k))
            send_near(t + WINDOW)
        if t >= LAG:
            kind, q = steps[t - LAG]
            arrived([far[kind, q]])
            compute(kind, q)
        if t == ZA:
            over_z_one()
        if t == ZB:
            over_z_two()

    back.append(send(vacc.at[pl.ds(128, 128)], VS, sib))
    arrived(back)
    total = vacc[:128] + VS[...]
    val_ref[...] = total.astype(bf16)
    mean = jnp.sum(gv_ref[...].astype(f32) * total, axis=1, keepdims=True) * (1.0 / 8192)

    mean_ref[...] = mean
    inv_ref[...] = inv
    for copy in sent:
        copy.wait_send()


WINDOW, LAG, ZA, ZB = 4, 5, 3, 11
N_COPIES = 3 + 6 + 15 + 4 + 2 + 6 + 6 + 16 + 4 + 7 + 8 + 7


def finish(
    tok_ref, gain_ref, gn_ref, inv_ref, mean_ref, sg_ref, occ_ref, val_ref, old_ref, m1_ref, m2_ref,
    val_out, gx_out, new_ref, n1_ref, n2_ref,
    gx, sem,
):
    inv, mean = inv_ref[...], mean_ref[...]
    copies = []
    for n in range(8):
        for s in (2 * n, 2 * n + 1):
            for h in range(2):
                cols = slice(512 * s + 256 * h, 512 * s + 256 * h + 256)
                weighted = gain_ref[:, cols] * gn_ref[s // 8, (s // 2) % 4, s % 2, h].astype(f32)
                scaled = tok_ref[:, cols].astype(f32) * inv
                gx[:, cols] = (inv * (weighted - scaled * mean)).astype(bf16)
        cols = pl.ds(1024 * n, 1024)
        copies.append(pltpu.make_async_copy(gx.at[:, cols], gx_out.at[:, cols], sem.at[n]))
        copies[-1].start()
    val_out[...] = val_ref[...]
    occupied, grad = occ_ref[:, :1], sg_ref[...]
    moment1 = (beta_one * m1_ref[...] + (1.0 - beta_one) * grad) * occupied
    moment2 = (beta_two * m2_ref[...] + (1.0 - beta_two) * grad * grad) * occupied
    step_dir = moment1 / bias_one / (jnp.sqrt(moment2 / bias_two) + adam_eps)
    new_ref[...] = (old_ref[...] - learn_rate * step_dir) * occupied
    n1_ref[...] = moment1
    n2_ref[...] = moment2
    for copy in copies:
        copy.wait()


def on_device(tokens, gain, w_t, grad_values, owner, master, moment1, moment2):
    vmem = pl.BlockSpec(memory_space=pltpu.VMEM)
    hbm = pl.BlockSpec(memory_space=pltpu.HBM)

    def far(array):
        return pltpu.with_memory_space_constraint(array, pltpu.HBM)

    values, grad_normed, tok, inv_rms, mean, slot_grad, occupied = pl.pallas_call(
        kernel,
        out_shape=(
            jax.ShapeDtypeStruct((128, 512), bf16),
            jax.ShapeDtypeStruct((2, 4, 2, 2, 128, 256), bf16),
            jax.ShapeDtypeStruct((128, 8192), bf16),
            jax.ShapeDtypeStruct((128, 1), f32),
            jax.ShapeDtypeStruct((128, 1), f32),
            jax.ShapeDtypeStruct((32, 512), f32),
            jax.ShapeDtypeStruct((32, 128), f32),
        ),
        in_specs=[hbm] * 5,
        out_specs=(vmem,) * 7,
        scratch_shapes=[
            pltpu.VMEM((1, 8192), f32),
            pltpu.VMEM((128, 512), bf16),
            pltpu.VMEM((1, 512), jnp.int32),
            pltpu.VMEM((2, 4, 2, 2, 4, 4, 2, 16, 256), bf16),
            pltpu.VMEM((2, 4, 2, 2, 2, 128, 128), bf16),
            pltpu.VMEM((2, 4, 2, 2, 128, 128), bf16),
            pltpu.VMEM((4, 2, 128, 512), bf16),
            pltpu.VMEM((4, 2, 128, 512), bf16),
            pltpu.VMEM((2, 2, 4, 2, 128, 128), bf16),
            pltpu.VMEM((4, 4, 2, 128, 128), bf16),
            pltpu.VMEM((4, 128, 512), bf16),
            pltpu.VMEM((4, 128, 512), bf16),
            pltpu.VMEM((3, 128, 512), bf16),
            pltpu.VMEM((3, 128, 512), bf16),
            pltpu.VMEM((1024, 512), bf16),
            pltpu.VMEM((4, 256, 256), bf16),
            pltpu.VMEM((3, 256, 256), bf16),
            pltpu.VMEM((4, 2, 32, 256), bf16),
            pltpu.VMEM((4, 2, 32, 256), bf16),
            pltpu.VMEM((2, 4, 2, 128, 256), bf16),
            pltpu.VMEM((256, 512), f32),
            pltpu.VMEM((128, 512), f32),
            pltpu.SemaphoreType.DMA((9,)),
            pltpu.SemaphoreType.DMA((N_COPIES,)),
            pltpu.SemaphoreType.DMA((N_COPIES,)),
            pltpu.SemaphoreType.REGULAR,
        ],
        compiler_params=pltpu.CompilerParams(
            collective_id=0, has_side_effects=True, vmem_limit_bytes=40 * 1024 * 1024
        ),
    )(far(tokens[0]), far(gain[None]), far(w_t), far(grad_values[0]), far(owner[None]))

    state = jax.ShapeDtypeStruct((32, 512), f32)
    values, grad_x, new_master, new_moment1, new_moment2 = pl.pallas_call(
        finish,
        out_shape=(
            jax.ShapeDtypeStruct((128, 512), bf16),
            jax.ShapeDtypeStruct((128, 8192), bf16),
            state,
            state,
            state,
        ),
        in_specs=[vmem] * 11,
        out_specs=(vmem, hbm, vmem, vmem, vmem),
        scratch_shapes=[pltpu.VMEM((128, 8192), bf16), pltpu.SemaphoreType.DMA((8,))],
        compiler_params=pltpu.CompilerParams(vmem_limit_bytes=8 * 1024 * 1024),
    )(tok, gain[None], grad_normed, inv_rms, mean, slot_grad, occupied, values, master[0], moment1[0], moment2[0])
    return (values[None], grad_x[None], new_master[None], new_moment1[None], new_moment2[None])


def solution(mesh):
    placed = (
        P("dp", "seq", None),
        P(),
        P("dp", "seq"),
        P("dp", "seq", None),
        P(),
        P("dp", None, "seq"),
        P("dp", None, "seq"),
        P("dp", None, "seq"),
    )
    return jax.shard_map(
        on_device,
        mesh=mesh,
        in_specs=placed,
        out_specs=(
            P("dp", "seq", None),
            P("dp", "seq", None),
            P("dp", None, "seq"),
            P("dp", None, "seq"),
            P("dp", None, "seq"),
        ),
        check_vma=False,
    )
```
